128 devices in a mesh: ens: 8 (over z_lo, y), lat: 16 (over x, z_hi, core).
Axes of the slice: x: 4, y: 4, z: 4 (z_hi: 2, z_lo: 2; z = z_hi * 2 + z_lo), core: 2. Of those that a mesh axis runs over, the one named last changes fastest.
Arguments:
- prediction_array: float32 [16, 16, 128, 1440], P('ens', None, 'lat'), may hold values from -6 to 6
- verifying_analysis: float32 [16, 128, 1440], P('ens', 'lat'), may hold values from -6 to 6
- variable_penalty_factor: float32 [16], replicated, may hold values from 0.25 to 4
Outputs:
- field_grad: float32 [16, 16, 128, 1440], P('ens', None, 'lat')
The draws below stay inside these ranges and needn't reach their ends.
All inputs are finite; a program needn't handle non-finite values.
Results may differ from the reference program's by a relative error of at most 0.00002.
Values sent between devices are 32-bit elements; how exact they have to be, the bound alone decides.
No kernel may reach another device: no remote copies, remote signals or barrier semaphores. Data moves between devices by JAX's collectives and lax.ppermute only.
A program may use at most 64 MiB of HBM per device.

```python
import math
import jax
import jax.numpy as jnp
from jax import lax

ENSEMBLE_SIZE = 16
VARIABLE_NUMBER = 16
MERIDIAN_NUMBER = 1440
COARSE = 3
PARALLEL_NUMBER = 128


def block_levels(rng, extent, cuts, low, top_value):
    loudness, own = 1.0, jax.random.fold_in(rng, 6)
    for axis_at, blocks in cuts:
        heights = jnp.exp(jax.random.uniform(jax.random.fold_in(own, axis_at), (blocks,), jnp.float32, low / len(cuts), top_value / len(cuts)))
        loudness = loudness * jnp.repeat(heights, extent[axis_at] // blocks).reshape([-1 if axis == axis_at else 1 for axis in range(len(extent))])
    return loudness


def normal_values(own_key, dims, spread, limit, cuts=(), held_as=jnp.bfloat16):
    array = jax.random.normal(own_key, dims, jnp.float32) * spread
    if len(cuts) > 0:
        array = block_levels(own_key, dims, cuts, -0.22, 0.18) * array
    return jnp.clip(array, min=-limit, max=limit).astype(held_as)


def setup_inputs(seed: int = 0) -> dict:
    splits = jax.random.split(jax.random.key(seed), 4)
    prediction_array = normal_values(splits[0], (ENSEMBLE_SIZE, VARIABLE_NUMBER, PARALLEL_NUMBER, MERIDIAN_NUMBER), 1.0, 6.0, ((0, 8), (2, 16)), jnp.float32)
    verifying_analysis = normal_values(splits[1], (VARIABLE_NUMBER, PARALLEL_NUMBER, MERIDIAN_NUMBER), 1.0, 6.0, ((0, 8), (1, 16)), jnp.float32)
    variable_penalty_factor = jnp.clip(jnp.exp(jax.random.uniform(splits[2], (VARIABLE_NUMBER,), jnp.float32, math.log(0.25), math.log(4.0))), 0.25, 4.0)
    return dict(prediction_array=prediction_array, verifying_analysis=verifying_analysis, variable_penalty_factor=variable_penalty_factor)


def normal_kernel_smoother(field):
    widths = [(0, 0)] * (field.ndim - 2) + [(1, 1), (0, 0)]
    padded = jnp.pad(field, widths)
    along = 0.25 * padded[..., :-2, :] + 0.5 * padded[..., 1:-1, :] + 0.25 * padded[..., 2:, :]
    return 0.25 * jnp.roll(along, 1, -1) + 0.5 * along + 0.25 * jnp.roll(along, -1, -1)

def slope(differ):
    return differ * lax.rsqrt(differ * differ + 0.01)

def couple_derivative(smooth_fc, smooth_obs, penalty_factor):
    count = smooth_fc.shape[0]

    def single(member):
        return lax.optimization_barrier(jnp.sum(slope(member[None] - smooth_fc), axis=0))
    pulls = lax.map(single, smooth_fc)
    return penalty_factor * (slope(smooth_fc - smooth_obs[None]) - 0.95 / (count - 1) * pulls)

def reference(prediction_array, verifying_analysis, variable_penalty_factor):
    sharp_prediction = normal_kernel_smoother(prediction_array)
    smooth_prediction = sharp_prediction
    sharp_analysis = normal_kernel_smoother(verifying_analysis)
    coarse_obs = sharp_analysis
    for repeat in range(COARSE - 1):
        smooth_prediction = normal_kernel_smoother(smooth_prediction)
        coarse_obs = normal_kernel_smoother(coarse_obs)
    rows_all = jnp.arange(PARALLEL_NUMBER).astype(jnp.float32)
    degrees = 0.25 * (rows_all - (PARALLEL_NUMBER - 1) / 2.0)
    lat_weight = jnp.cos(jnp.deg2rad(degrees))
    penalty_factor = variable_penalty_factor[:, None, None] * lat_weight[None, :, None]
    sharp_derivative = couple_derivative(sharp_prediction, sharp_analysis, penalty_factor)
    grad_coarse = couple_derivative(smooth_prediction, coarse_obs, penalty_factor)
    level = grad_coarse
    for repeat in range(COARSE - 1):
        level = normal_kernel_smoother(level)
    return normal_kernel_smoother(sharp_derivative + level)
```

```python
import functools

import jax
import jax.numpy as jnp
import numpy as np
from jax import lax
from jax.experimental import pallas as pl
from jax.experimental.pallas import tpu as pltpu
from jax.sharding import PartitionSpec as P

MEMBERS, CHANNELS, ROWS, COLS = 16, 16, 128, 1440
BLOCKS = 8
BLOCK = COLS // BLOCKS
LANES, SIDE, HALO = 128, 64, 6
PAIRS = MEMBERS // 2
RC = 8
PAD = 8
SHARE = 0.95 / (MEMBERS - 1)
FINE = (0.5, 0.25)
COARSE = (20 / 64, 15 / 64, 6 / 64, 1 / 64)
VMEM = pl.BlockSpec(memory_space=pltpu.VMEM)
SMEM = pl.BlockSpec(memory_space=pltpu.SMEM)


def offset_of(block):
    return (BLOCK * block - HALO) % LANES


def lane_ids(shape=(RC, LANES)):
    return lax.broadcasted_iota(jnp.int32, shape, len(shape) - 1)


def column_runs(wanted):
    runs = []
    for lane, col in wanted:
        if runs:
            p, q, n = runs[-1]
            if p + n == lane and q + n == col and col % LANES:
                runs[-1] = (p, q, n + 1)
                continue
        runs.append((lane, col, 1))
    return runs


def gather_tile(load, parts, lanes):
    tile = None
    for source, p, q, n in parts:
        base = min(q // LANES * LANES, COLS - LANES)
        piece = load(source, base)
        shift = (p - (q - base)) % LANES
        if shift:
            piece = pltpu.roll(piece, shift, 1)
        tile = piece if tile is None else jnp.where((lanes >= p) & (lanes < p + n), piece, tile)
    return tile


def main_parts(source, block):
    o = offset_of(block)
    lanes = sorted(range(LANES), key=lambda j: (j + o) % LANES)
    runs = column_runs([((j + o) % LANES, (BLOCK * block - HALO + j) % COLS) for j in lanes])
    return [(source, p, q, n) for p, q, n in runs]


def side_parts(first, second, block):
    o = offset_of(block)
    parts = []
    for source, half in ((first, 0), (second, 1)):
        wanted = [
            ((r + o) % LANES, (BLOCK * block - HALO + LANES + r % SIDE) % COLS)
            for r in range(half * SIDE, (half + 1) * SIDE)
        ]
        parts += [(source, p, q, n) for p, q, n in column_runs(sorted(wanted))]
    return parts


def pack_kernel(x_ref, obs_ref, msg_ref, obs_msg_ref):
    lanes = lane_ids()

    def load_obs(source, base):
        return obs_ref[source, :, base : base + LANES]

    for h in range(2):
        for b in range(BLOCKS):
            obs_msg_ref[h * BLOCKS + b, 0] = gather_tile(load_obs, main_parts(h, b), lanes)
            obs_msg_ref[h * BLOCKS + b, 1] = gather_tile(load_obs, side_parts(h, h, b), lanes)

    def channel(c, carry):
        def load(source, base):
            return x_ref[source, c, :, base : base + LANES]

        for b in range(BLOCKS):
            dst = c * BLOCKS + b
            msg_ref[dst, 0] = gather_tile(load, main_parts(0, b), lanes)
            msg_ref[dst, 1] = gather_tile(load, main_parts(1, b), lanes)
            msg_ref[dst, 2] = gather_tile(load, side_parts(0, 1, b), lanes)
        return carry

    lax.fori_loop(0, CHANNELS, channel, 0)


def unpack_kernel(ret_ref, out_ref):
    lanes = lane_ids()

    def channel(c, carry):
        for m in range(2):
            for t in range((COLS + LANES - 1) // LANES):
                tile = None
                q = t * LANES
                end = min(q + LANES, COLS)
                while q < end:
                    b, k = q // BLOCK, q % BLOCK
                    stop = b * BLOCK + (BLOCK - SIDE if k < BLOCK - SIDE else BLOCK)
                    src = c * BLOCKS + b
                    if k < BLOCK - SIDE:
                        piece = ret_ref[src, m]
                    else:
                        piece = ret_ref[src, 2]
                        if m:
                            piece = pltpu.roll(piece, SIDE, 1)
                    p = q - t * LANES
                    tile = piece if tile is None else jnp.where(lanes >= p, piece, tile)
                    q = min(stop, end)
                if end - t * LANES == LANES:
                    out_ref[m, c, :, t * LANES : end] = tile
                else:
                    out_ref[m, c, :, t * LANES : end] = tile[:, : end - t * LANES]
        return carry

    lax.fori_loop(0, CHANNELS, channel, 0)


def taps(distance, weights):
    value = jnp.zeros(distance.shape, jnp.float32)
    for d, w in enumerate(weights):
        value = jnp.where(distance == d, w, value)
    return value


def matrices_kernel(o_ref, main_ref, side_ref, back_a_ref, back_b_ref, back_s_ref):
    o = o_ref[0]
    shape = (LANES, LANES)
    row = lax.broadcasted_iota(jnp.int32, shape, 0)
    col = lax.broadcasted_iota(jnp.int32, shape, 1)
    turned_row = (row - o) & (LANES - 1)
    turned_col = (col - o) & (LANES - 1)
    far = 99
    valid_col = (col >= 3) & (col < LANES - 3)
    valid_row = (row >= 3) & (row < LANES - 3)

    def put(ref, start, lane, distance, weights):
        tile = taps(distance, weights).astype(jnp.bfloat16)
        for i in range(3):
            ref[start + i * LANES : start + (i + 1) * LANES, lane : lane + LANES] = tile

    first_col = col < SIDE
    target_pair = jnp.where(first_col, col + (LANES - 3), col + (LANES - 3 - SIDE))
    first_turned = turned_row < SIDE
    source_side = jnp.where(first_turned, turned_row + LANES, turned_row + (LANES - SIDE))
    for s, weights in enumerate((FINE, COARSE)):
        lane = s * LANES
        put(main_ref, 0, lane, jnp.where(valid_col, jnp.abs(turned_row - col), far), weights)
        near = jnp.abs(turned_row - target_pair)
        put(side_ref, 0, lane, jnp.where(first_col, near, far), weights)
        same = first_turned == first_col
        put(side_ref, 3 * LANES, lane, jnp.where(same, jnp.abs(source_side - target_pair), far), weights)
        put(side_ref, 6 * LANES, lane, jnp.where(first_col, far, near), weights)

    out_main = (turned_col >= HALO) & (turned_col < LANES - HALO)
    out_second = (turned_col >= SIDE - HALO) & (turned_col < LANES - HALO)
    target_side = jnp.where(
        out_second, turned_col + SIDE, jnp.where(turned_col < SIDE, turned_col + LANES, turned_col)
    )
    row_first = row < SIDE
    source_pair = jnp.where(row_first, row + (LANES - 3), row + (LANES - 3 - SIDE))
    for s, weights in enumerate((FINE, COARSE)):
        start = s * 3 * LANES
        near = jnp.where(valid_row & out_main, jnp.abs(row - turned_col), far)
        cross = jnp.where(valid_row, jnp.abs(row - target_side), far)
        put(back_a_ref, start, 0, near, weights)
        put(back_a_ref, start, LANES, jnp.where(out_second, far, cross), weights)
        put(back_b_ref, start, 0, near, weights)
        put(back_b_ref, start, LANES, jnp.where(out_second, cross, far), weights)
        same = row_first == jnp.logical_not(out_second)
        put(back_s_ref, start, 0, jnp.where(same, jnp.abs(source_pair - target_side), far), weights)


def thirds(x):
    high = x.astype(jnp.bfloat16)
    rest = x - high.astype(jnp.float32)
    middle = rest.astype(jnp.bfloat16)
    low = (rest - middle.astype(jnp.float32)).astype(jnp.bfloat16)
    return [high, middle, low]


def times(parts, matrix):
    return jnp.dot(jnp.concatenate(parts, axis=1), matrix, preferred_element_type=jnp.float32)


def fine_rows(ref, i, start, size):
    at = lambda d: ref[i, pl.ds(start + PAD + d, size), :]
    return 0.25 * (at(-1) + at(1)) + 0.5 * at(0)


def coarse_rows(ref, i, start, size):
    at = lambda d: ref[i, pl.ds(start + PAD + d, size), :]
    return (
        (at(-3) + at(3)) * COARSE[3]
        + (at(-2) + at(2)) * COARSE[2]
        + (at(-1) + at(1)) * COARSE[1]
        + at(0) * COARSE[0]
    )


def mirror(ref, i):
    end = PAD + ROWS
    for outside, inside in ((PAD - 2, PAD), (PAD - 3, PAD + 1), (end + 1, end - 1), (end + 2, end - 2)):
        ref[i, outside : outside + 1, :] = -ref[i, inside : inside + 1, :]


def slope(d):
    return d * lax.rsqrt(d * d + 0.01)


def work_kernel(
    factor_ref, got_ref, obs_ref, lat_ref, main_ref, side_ref, back_a_ref, back_b_ref, back_s_ref,
    out_ref, fine_ref, coarse_ref, gfine_ref, gcoarse_ref,
):
    zeros = jnp.zeros((PAD, LANES), jnp.float32)

    def clear(i, carry):
        for ref in (fine_ref, coarse_ref):
            ref[i, 0:PAD, :] = zeros
            ref[i, PAD + ROWS : 2 * PAD + ROWS, :] = zeros
        return carry

    lax.fori_loop(0, 3 * PAIRS + 2, clear, 0)

    def clear_back(i, carry):
        for ref in (gfine_ref, gcoarse_ref):
            ref[i, 0:PAD, :] = zeros
            ref[i, PAD + ROWS : 2 * PAD + ROWS, :] = zeros
        return carry

    lax.fori_loop(0, 3 * PAIRS, clear_back, 0)

    def keep(i, both):
        fine_ref[i, PAD : PAD + ROWS, :] = both[:, :LANES]
        coarse_ref[i, PAD : PAD + ROWS, :] = both[:, LANES:]
        mirror(coarse_ref, i)

    def forward(p, carry):
        a, b, s = (thirds(got_ref[p, :, t].reshape(ROWS, LANES)) for t in range(3))
        keep(3 * p, times(a, main_ref[...]))
        keep(3 * p + 1, times(b, main_ref[...]))
        keep(3 * p + 2, times(a + s + b, side_ref[...]))
        return carry

    lax.fori_loop(0, PAIRS, forward, 0)
    a, s = (thirds(obs_ref[:, t].reshape(ROWS, LANES)) for t in range(2))
    keep(3 * PAIRS, times(a, main_ref[...]))
    keep(3 * PAIRS + 1, times(a + s + a, side_ref[...]))

    factor = factor_ref[0]

    def pull(n, carry):
        start = pl.multiple_of(n * RC, RC)
        weight = jnp.broadcast_to(lat_ref[pl.ds(start, RC), :] * factor, (RC, LANES))
        for rows, ref, gref in ((fine_rows, fine_ref, gfine_ref), (coarse_rows, coarse_ref, gcoarse_ref)):
            mains = [3 * (m // 2) + m % 2 for m in range(MEMBERS)]
            value = [rows(ref, i, start, RC) for i in mains]
            total = [None] * MEMBERS
            for m in range(MEMBERS):
                for k in range(m + 1, MEMBERS):
                    part = slope(value[m] - value[k])
                    total[m] = part if total[m] is None else total[m] + part
                    total[k] = -part if total[k] is None else total[k] - part
            target = rows(ref, 3 * PAIRS, start, RC)
            for m, i in enumerate(mains):
                grad = weight * (slope(value[m] - target) - SHARE * total[m])
                gref[i, pl.ds(start + PAD, RC), :] = grad

            value = [rows(ref, 3 * p + 2, start, RC) for p in range(PAIRS)]
            other = [pltpu.roll(v, SIDE, 1) for v in value]
            total = [slope(value[p] - other[p]) for p in range(PAIRS)]
            swapped = [None] * PAIRS
            for p in range(PAIRS):
                for k in range(p + 1, PAIRS):
                    part = slope(value[p] - value[k])
                    cross = slope(value[p] - other[k])
                    total[p] = total[p] + (part + cross)
                    total[k] = total[k] - part
                    swapped[k] = -cross if swapped[k] is None else swapped[k] - cross
            target = rows(ref, 3 * PAIRS + 1, start, RC)
            for p in range(PAIRS):
                full = total[p] if swapped[p] is None else total[p] + pltpu.roll(swapped[p], SIDE, 1)
                grad = weight * (slope(value[p] - target) - SHARE * full)
                gref[3 * p + 2, pl.ds(start + PAD, RC), :] = grad
        return carry

    lax.fori_loop(0, ROWS // RC, pull, 0)

    def backward(p, carry):
        def rows_of(i):
            mirror(gcoarse_ref, i)
            return thirds(fine_rows(gfine_ref, i, 0, ROWS)) + thirds(coarse_rows(gcoarse_ref, i, 0, ROWS))

        first = times(rows_of(3 * p), back_a_ref[...])
        second = times(rows_of(3 * p + 1), back_b_ref[...])
        side = times(rows_of(3 * p + 2), back_s_ref[...])
        blocks = (ROWS // RC, RC, LANES)
        out_ref[p, :, 0] = first[:, :LANES].reshape(blocks)
        out_ref[p, :, 1] = second[:, :LANES].reshape(blocks)
        out_ref[p, :, 2] = (side + first[:, LANES:] + second[:, LANES:]).reshape(blocks)
        return carry

    lax.fori_loop(0, PAIRS, backward, 0)


def shape(*dims, dtype=jnp.float32):
    return jax.ShapeDtypeStruct(dims, dtype)


def body(prediction_array, verifying_analysis, variable_penalty_factor):
    ens, lat = lax.axis_index("ens"), lax.axis_index("lat")
    block = lat % BLOCKS
    channel = 2 * ens + lat // BLOCKS
    offset = ((BLOCK * block - HALO) % LANES).astype(jnp.int32).reshape(1)
    factor = lax.dynamic_slice_in_dim(variable_penalty_factor, channel, 1)
    degrees = 0.25 * (np.arange(ROWS, dtype=np.float32) - (ROWS - 1) / 2.0)
    lat_weight = jnp.asarray(np.cos(np.deg2rad(degrees)).astype(np.float32)[:, None])

    msg, obs_msg = pl.pallas_call(
        pack_kernel,
        out_shape=(shape(128, 3, RC, LANES), shape(16, 2, RC, LANES)),
        in_specs=[VMEM, VMEM],
        out_specs=(VMEM, VMEM),
        name="pack",
    )(prediction_array, verifying_analysis)
    bf = jnp.bfloat16
    mats = pl.pallas_call(
        matrices_kernel,
        out_shape=(
            shape(3 * LANES, 2 * LANES, dtype=bf),
            shape(9 * LANES, 2 * LANES, dtype=bf),
            shape(6 * LANES, 2 * LANES, dtype=bf),
            shape(6 * LANES, 2 * LANES, dtype=bf),
            shape(6 * LANES, LANES, dtype=bf),
        ),
        in_specs=[SMEM],
        out_specs=(VMEM,) * 5,
        name="matrices",
        cost_estimate=pl.CostEstimate(flops=10_000_000, bytes_accessed=1_000_000, transcendentals=0),
    )(offset)
    obs_got = lax.all_to_all(obs_msg, "lat", 0, 0, tiled=True)
    got = lax.all_to_all(msg, ("ens", "lat"), 0, 0, tiled=True)
    padded = (ROWS + 2 * PAD, LANES)
    back = pl.pallas_call(
        work_kernel,
        out_shape=shape(PAIRS, ROWS // RC, 3, RC, LANES),
        in_specs=[SMEM] + [VMEM] * 8,
        out_specs=VMEM,
        scratch_shapes=[
            pltpu.VMEM((3 * PAIRS + 2, *padded), jnp.float32),
            pltpu.VMEM((3 * PAIRS + 2, *padded), jnp.float32),
            pltpu.VMEM((3 * PAIRS, *padded), jnp.float32),
            pltpu.VMEM((3 * PAIRS, *padded), jnp.float32),
        ],
        name="work",
    )(factor, got.reshape(PAIRS, ROWS // RC, 3, RC, LANES), obs_got, lat_weight, *mats)
    ret = lax.all_to_all(back.reshape(128, 3, RC, LANES), ("ens", "lat"), 0, 0, tiled=True)
    return pl.pallas_call(
        unpack_kernel,
        out_shape=shape(2, CHANNELS, RC, COLS),
        in_specs=[VMEM],
        out_specs=VMEM,
        name="unpack",
    )(ret)


def solution(mesh):
    placed = (P("ens", None, "lat", None), P("ens", "lat", None), P())
    return jax.shard_map(
        body, mesh=mesh, in_specs=placed, out_specs=P("ens", None, "lat", None), check_vma=False
    )
```

```python
import jax
import jax.numpy as jnp
import numpy as np
from jax import lax
from jax.experimental import pallas as pl
from jax.experimental.pallas import tpu as pltpu
from jax.sharding import PartitionSpec as P

MEMBERS, CHANNELS, ROWS, COLS = 16, 16, 128, 1440
BLOCKS = 8
BLOCK = COLS // BLOCKS
LANES, SIDE, HALO = 128, 64, 6
PAIRS = MEMBERS // 2
RC = 8
PAD = 8
LATS = 16
SHARE = 0.95 / (MEMBERS - 1)
FINE_SCALE, COARSE_SCALE = 16.0, 4096.0
VMEM = pl.BlockSpec(memory_space=pltpu.VMEM)
SMEM = pl.BlockSpec(memory_space=pltpu.SMEM)


def offset_of(block):
    return (BLOCK * block + LANES - HALO) % LANES


def lane_ids(shape=(RC, LANES)):
    return lax.broadcasted_iota(jnp.int32, shape, len(shape) - 1)


def column_runs(wanted):
    runs = []
    for lane, col in wanted:
        if runs:
            p, q, n = runs[-1]
            if p + n == lane and q + n == col and col % LANES:
                runs[-1] = (p, q, n + 1)
                continue
        runs.append((lane, col, 1))
    return runs


def gather_tile(load, parts, lanes):
    tile = None
    for source, p, q, n in parts:
        base = min(q // LANES * LANES, COLS - LANES)
        piece = load(source, base)
        shift = (p - (q - base)) % LANES
        if shift:
            piece = pltpu.roll(piece, shift, 1)
        tile = piece if tile is None else jnp.where((lanes >= p) & (lanes < p + n), piece, tile)
    return tile


def main_parts(source, block):
    o = offset_of(block)
    lanes = sorted(range(LANES), key=lambda j: (j + o) % LANES)
    runs = column_runs([((j + o) % LANES, (BLOCK * block - HALO + j) % COLS) for j in lanes])
    return [(source, p, q, n) for p, q, n in runs]


def side_parts(first, second, block):
    o = offset_of(block)
    parts = []
    for source, half in ((first, 0), (second, 1)):
        wanted = [
            ((r + o) % LANES, (BLOCK * block - HALO + LANES + r % SIDE) % COLS)
            for r in range(half * SIDE, (half + 1) * SIDE)
        ]
        parts += [(source, p, q, n) for p, q, n in column_runs(sorted(wanted))]
    return parts


def pack_obs_kernel(lat_ref, obs_ref, obs_msg_ref):
    lanes = lane_ids()
    me = lat_ref[0]

    def load_obs(source, base):
        return obs_ref[source, :, base : base + LANES]

    for h in range(2):
        for b in range(BLOCKS):
            slot = me ^ (h * BLOCKS + b)
            obs_msg_ref[slot, 0] = gather_tile(load_obs, main_parts(h, b), lanes)
            obs_msg_ref[slot, 1] = gather_tile(load_obs, side_parts(h, h, b), lanes)


def pack_kernel(x_ref, msg_ref):
    lanes = lane_ids()

    def channel(c, carry):
        def load(source, base):
            return x_ref[source, c, :, base : base + LANES]

        for b in range(BLOCKS):
            dst = c * BLOCKS + b
            msg_ref[dst, 0] = gather_tile(load, main_parts(0, b), lanes)
            msg_ref[dst, 1] = gather_tile(load, main_parts(1, b), lanes)
            msg_ref[dst, 2] = gather_tile(load, side_parts(0, 1, b), lanes)
        return carry

    lax.fori_loop(0, x_ref.shape[1], channel, 0)


def unpack_kernel(ret_ref, out_ref):
    lanes = lane_ids()

    def channel(c, carry):
        for m in range(2):
            for t in range((COLS + LANES - 1) // LANES):
                tile = None
                q = t * LANES
                end = min(q + LANES, COLS)
                while q < end:
                    b, k = q // BLOCK, q % BLOCK
                    stop = b * BLOCK + (BLOCK - SIDE if k < BLOCK - SIDE else BLOCK)
                    src = c * BLOCKS + b
                    if k < BLOCK - SIDE:
                        piece = ret_ref[src, m]
                    else:
                        piece = ret_ref[src, 2]
                        if m:
                            piece = pltpu.roll(piece, SIDE, 1)
                    p = q - t * LANES
                    tile = piece if tile is None else jnp.where(lanes >= p, piece, tile)
                    q = min(stop, end)
                if end - t * LANES == LANES:
                    out_ref[m, c, :, t * LANES : end] = tile
                else:
                    out_ref[m, c, :, t * LANES : end] = tile[:, : end - t * LANES]
        return carry

    lax.fori_loop(0, out_ref.shape[1], channel, 0)


def along_lon(x):
    t = x + pltpu.roll(x, 1, 1)
    return t + pltpu.roll(t, LANES - 1, 1)


def along_lat(x, ref, i):
    ref[i, PAD : PAD + ROWS, :] = x
    return (ref[i, PAD - 1 : PAD - 1 + ROWS, :] + ref[i, PAD + 1 : PAD + 1 + ROWS, :]) + (x + x)


def slope(d, floor):
    return d * lax.rsqrt(d * d + floor)


def work_kernel(
    ens_ref, lat_ref, factor_ref, weight_ref, got_ref, obs_ref,
    out_ref, fine_ref, coarse_ref, gfine_ref, gcoarse_ref, rows_ref,
):
    me = lat_ref[0]
    block = me & (BLOCKS - 1)
    factor = factor_ref[2 * ens_ref[0] + (me >> 3)]
    offset = BLOCK * block + LANES - HALO
    turned = (lane_ids((ROWS, LANES)) - offset) & (LANES - 1)
    upper = turned >= SIDE
    inner = (turned >= LANES - 3) | (turned < SIDE - 3)
    outer = (turned >= LANES - HALO) | (turned < SIDE - HALO)
    zeros = jnp.zeros((PAD, LANES), jnp.float32)
    for i in range(rows_ref.shape[0]):
        rows_ref[i, 0:PAD, :] = zeros
        rows_ref[i, PAD + ROWS : 2 * PAD + ROWS, :] = zeros

    def both_scales(x, i):
        fine = along_lat(along_lon(x), rows_ref, 3 * i)
        twice = along_lat(along_lon(fine), rows_ref, 3 * i + 1)
        return fine, along_lat(along_lon(twice), rows_ref, 3 * i + 2)

    def join(a, b):
        return jnp.where(inner, a, pltpu.roll(b, SIDE, 1))

    def forward(p, carry):
        a, b, s = (got_ref[p, :, t].reshape(ROWS, LANES) for t in range(3))
        first = both_scales(a, 0)
        second = both_scales(b, 1)
        side_a = both_scales(jnp.where(upper, a, s), 2)
        side_b = both_scales(jnp.where(upper, b, pltpu.roll(s, SIDE, 1)), 3)
        for s, ref in enumerate((fine_ref, coarse_ref)):
            ref[3 * p] = first[s]
            ref[3 * p + 1] = second[s]
            ref[3 * p + 2] = join(side_a[s], side_b[s])
        return carry

    lax.fori_loop(0, PAIRS, forward, 0)
    a, s = (
        jnp.concatenate([obs_ref[me ^ l, t] for l in range(LATS)], axis=0) for t in range(2)
    )
    first = both_scales(a, 0)
    side = both_scales(jnp.where(upper, a, s), 1)
    for s, ref in enumerate((fine_ref, coarse_ref)):
        ref[3 * PAIRS] = first[s]
        ref[3 * PAIRS + 1] = join(side[s], side[s])

    def pull(n, carry):
        start = pl.multiple_of(n * RC, RC)
        here = pl.ds(start, RC)
        row_weight = jnp.broadcast_to(weight_ref[here, :] * factor, (RC, LANES))
        for ref, gref, scale in ((fine_ref, gfine_ref, FINE_SCALE), (coarse_ref, gcoarse_ref, COARSE_SCALE)):
            floor = 0.01 * scale * scale
            weight = row_weight * (1.0 / scale)
            shared = weight * SHARE
            mains = [3 * (m // 2) + m % 2 for m in range(MEMBERS)]
            value = [ref[i, here, :] for i in mains]
            total = [None] * MEMBERS
            for m in range(MEMBERS):
                for k in range(m + 1, MEMBERS):
                    part = slope(value[m] - value[k], floor)
                    total[m] = part if total[m] is None else total[m] + part
                    total[k] = -part if total[k] is None else total[k] - part
            target = ref[3 * PAIRS, here, :]
            for m, i in enumerate(mains):
                gref[i, here, :] = weight * slope(value[m] - target, floor) - shared * total[m]

            value = [ref[3 * p + 2, here, :] for p in range(PAIRS)]
            other = [pltpu.roll(v, SIDE, 1) for v in value]
            total = [slope(value[p] - other[p], floor) for p in range(PAIRS)]
            swapped = [None] * PAIRS
            for p in range(PAIRS):
                for k in range(p + 1, PAIRS):
                    part = slope(value[p] - value[k], floor)
                    cross = slope(value[p] - other[k], floor)
                    total[p] = total[p] + (part + cross)
                    total[k] = total[k] - part
                    swapped[k] = -cross if swapped[k] is None else swapped[k] - cross
            target = ref[3 * PAIRS + 1, here, :]
            for p in range(PAIRS):
                full = total[p] if swapped[p] is None else total[p] + pltpu.roll(swapped[p], SIDE, 1)
                gref[3 * p + 2, here, :] = weight * slope(value[p] - target, floor) - shared * full
        return carry

    lax.fori_loop(0, ROWS // RC, pull, 0)

    def adjoint(fine, coarse, i):
        once = along_lat(along_lon(coarse), rows_ref, 3 * i)
        twice = along_lat(along_lon(once), rows_ref, 3 * i + 1)
        return along_lat(along_lon(twice + fine), rows_ref, 3 * i + 2)

    def backward(p, carry):
        def split(ref):
            a, b, s = ref[3 * p], ref[3 * p + 1], ref[3 * p + 2]
            return a, b, jnp.where(inner, s, a), jnp.where(inner, pltpu.roll(s, SIDE, 1), b)

        a, b, side_a, side_b = (
            adjoint(f, c, i) for i, (f, c) in enumerate(zip(split(gfine_ref), split(gcoarse_ref)))
        )
        blocks = (ROWS // RC, RC, LANES)
        out_ref[p, :, 0] = a.reshape(blocks)
        out_ref[p, :, 1] = b.reshape(blocks)
        out_ref[p, :, 2] = jnp.where(outer, side_a, pltpu.roll(side_b, SIDE, 1)).reshape(blocks)
        return carry

    lax.fori_loop(0, PAIRS, backward, 0)


def shape(*dims):
    return jax.ShapeDtypeStruct(dims, jnp.float32)


def grant(mib):
    return pltpu.CompilerParams(vmem_limit_bytes=mib << 20)


def exchange_slots(slots):
    slots = slots.reshape(2, 2, 2, 2, *slots.shape[1:])
    for axis in range(4):
        step = 8 >> axis
        kept = lax.index_in_dim(slots, 0, axis, keepdims=True)
        sent = lax.index_in_dim(slots, 1, axis, keepdims=True)
        got = lax.ppermute(sent, "lat", [(i, i ^ step) for i in range(LATS)])
        slots = jnp.concatenate([kept, got], axis=axis)
    return slots.reshape(LATS, *slots.shape[4:])


def body(prediction_array, verifying_analysis, variable_penalty_factor):
    ens = lax.axis_index("ens").astype(jnp.int32).reshape(1)
    lat = lax.axis_index("lat").astype(jnp.int32).reshape(1)
    degrees = 0.25 * (np.arange(ROWS, dtype=np.float32) - (ROWS - 1) / 2.0)
    lat_weight = jnp.asarray(np.cos(np.deg2rad(degrees)).astype(np.float32)[:, None])

    msg = pl.pallas_call(
        pack_kernel,
        out_shape=shape(128, 3, RC, LANES),
        in_specs=[VMEM],
        out_specs=VMEM,
        compiler_params=grant(8),
        name="pack",
    )(prediction_array)
    got = lax.all_to_all(msg, ("ens", "lat"), 0, 0, tiled=True)
    obs_msg = pl.pallas_call(
        pack_obs_kernel,
        out_shape=shape(LATS, 2, RC, LANES),
        in_specs=[SMEM, VMEM],
        out_specs=VMEM,
        compiler_params=grant(2),
        name="pack_obs",
    )(lat, verifying_analysis)
    obs_got = exchange_slots(obs_msg)
    padded = (ROWS + 2 * PAD, LANES)
    back = pl.pallas_call(
        work_kernel,
        out_shape=shape(PAIRS, ROWS // RC, 3, RC, LANES),
        in_specs=[SMEM, SMEM, SMEM, VMEM, VMEM, VMEM],
        out_specs=VMEM,
        scratch_shapes=[
            pltpu.VMEM((3 * PAIRS + 2, ROWS, LANES), jnp.float32),
            pltpu.VMEM((3 * PAIRS + 2, ROWS, LANES), jnp.float32),
            pltpu.VMEM((3 * PAIRS, ROWS, LANES), jnp.float32),
            pltpu.VMEM((3 * PAIRS, ROWS, LANES), jnp.float32),
            pltpu.VMEM((12, *padded), jnp.float32),
        ],
        compiler_params=grant(16),
        name="work",
    )(ens, lat, variable_penalty_factor, lat_weight, got.reshape(PAIRS, ROWS // RC, 3, RC, LANES), obs_got)
    ret = lax.all_to_all(back.reshape(128, 3, RC, LANES), ("ens", "lat"), 0, 0, tiled=True)
    return pl.pallas_call(
        unpack_kernel,
        out_shape=shape(2, CHANNELS, RC, COLS),
        in_specs=[VMEM],
        out_specs=VMEM,
        compiler_params=grant(8),
        name="unpack",
    )(ret)


def solution(mesh):
    placed = (P("ens", None, "lat", None), P("ens", "lat", None), P())
    return jax.shard_map(
        body, mesh=mesh, in_specs=placed, out_specs=P("ens", None, "lat", None), check_vma=False
    )
```

```python
import jax
import jax.numpy as jnp
import numpy as np
from jax import lax
from jax.experimental import pallas as pl
from jax.experimental.pallas import tpu as pltpu
from jax.sharding import PartitionSpec as P

MEMBERS, CHANNELS, ROWS, COLS = 16, 16, 128, 1440
BLOCKS = 8
BLOCK = COLS // BLOCKS
LANES, SIDE, HALO = 128, 64, 6
PAIRS = MEMBERS // 2
RC = 8
PAD = 8
LATS = 16
SHARE = 0.95 / (MEMBERS - 1)
FINE, COARSE = (2, 1), (20, 15, 6, 1)
FINE_SCALE, COARSE_SCALE = 16.0, 4096.0
TURN, UNROLL = 2, 2
PACK = 4
VMEM = pl.BlockSpec(memory_space=pltpu.VMEM)
SMEM = pl.BlockSpec(memory_space=pltpu.SMEM)


def offset_of(block):
    return (BLOCK * block + LANES - HALO) % LANES


def lane_ids(shape=(RC, LANES)):
    return lax.broadcasted_iota(jnp.int32, shape, len(shape) - 1)


def column_runs(wanted):
    runs = []
    for lane, col in wanted:
        if runs:
            p, q, n = runs[-1]
            if p + n == lane and q + n == col and col % LANES:
                runs[-1] = (p, q, n + 1)
                continue
        runs.append((lane, col, 1))
    return runs


def gather_tile(load, parts, lanes):
    tile = None
    for source, p, q, n in parts:
        base = min(q // LANES * LANES, COLS - LANES)
        piece = load(source, base)
        shift = (p - (q - base)) % LANES
        if shift:
            piece = pltpu.roll(piece, shift, 1)
        tile = piece if tile is None else jnp.where((lanes >= p) & (lanes < p + n), piece, tile)
    return tile


def main_parts(source, block):
    o = offset_of(block)
    lanes = sorted(range(LANES), key=lambda j: (j + o) % LANES)
    runs = column_runs([((j + o) % LANES, (BLOCK * block - HALO + j) % COLS) for j in lanes])
    return [(source, p, q, n) for p, q, n in runs]


def side_parts(first, second, block):
    o = offset_of(block)
    parts = []
    for source, half in ((first, 0), (second, 1)):
        wanted = [
            ((r + o) % LANES, (BLOCK * block - HALO + LANES + r % SIDE) % COLS)
            for r in range(half * SIDE, (half + 1) * SIDE)
        ]
        parts += [(source, p, q, n) for p, q, n in column_runs(sorted(wanted))]
    return parts


def pack_obs_kernel(lat_ref, obs_ref, obs_msg_ref):
    lanes = lane_ids()
    me = lat_ref[0]

    def load_obs(source, base):
        return obs_ref[source, :, base : base + LANES]

    for h in range(2):
        for b in range(BLOCKS):
            slot = me ^ (h * BLOCKS + b)
            obs_msg_ref[slot, 0] = gather_tile(load_obs, main_parts(h, b), lanes)
            obs_msg_ref[slot, 1] = gather_tile(load_obs, side_parts(h, h, b), lanes)


def pack_kernel(x_ref, msg_ref):
    lanes = lane_ids()

    def channel(c, carry):
        def load(source, base):
            return x_ref[source, c, :, base : base + LANES]

        for b in range(BLOCKS):
            dst = c * BLOCKS + b
            msg_ref[dst, 0] = gather_tile(load, main_parts(0, b), lanes)
            msg_ref[dst, 1] = gather_tile(load, main_parts(1, b), lanes)
            msg_ref[dst, 2] = gather_tile(load, side_parts(0, 1, b), lanes)
        return carry

    lax.fori_loop(0, x_ref.shape[1], channel, 0)


def unpack_kernel(ret_ref, out_ref):
    lanes = lane_ids()

    def channel(c, carry):
        for m in range(2):
            for t in range((COLS + LANES - 1) // LANES):
                tile = None
                q = t * LANES
                end = min(q + LANES, COLS)
                while q < end:
                    b, k = q // BLOCK, q % BLOCK
                    stop = b * BLOCK + (BLOCK - SIDE if k < BLOCK - SIDE else BLOCK)
                    src = c * BLOCKS + b
                    if k < BLOCK - SIDE:
                        piece = ret_ref[src, m]
                    else:
                        piece = ret_ref[src, 2]
                        if m:
                            piece = pltpu.roll(piece, SIDE, 1)
                    p = q - t * LANES
                    tile = piece if tile is None else jnp.where(lanes >= p, piece, tile)
                    q = min(stop, end)
                if end - t * LANES == LANES:
                    out_ref[m, c, :, t * LANES : end] = tile
                else:
                    out_ref[m, c, :, t * LANES : end] = tile[:, : end - t * LANES]
        return carry

    lax.fori_loop(0, out_ref.shape[1], channel, 0)


def taps(distance, weights):
    value = jnp.zeros(distance.shape, jnp.float32)
    for d, w in enumerate(weights):
        value = jnp.where(distance == d, w, value)
    return value


def matrices_kernel(lat_ref, main_ref, side_ref, back_a_ref, back_b_ref, back_s_ref):
    offset = BLOCK * (lat_ref[0] & (BLOCKS - 1)) + LANES - HALO
    size = (LANES, LANES)
    row = lax.broadcasted_iota(jnp.int32, size, 0)
    col = lax.broadcasted_iota(jnp.int32, size, 1)
    turned_row = (row - offset) & (LANES - 1)
    turned_col = (col - offset) & (LANES - 1)
    far = 99

    def put(ref, start, lane, distance, weights):
        tile = taps(distance, weights).astype(jnp.bfloat16)
        for i in range(3):
            ref[start + i * LANES : start + (i + 1) * LANES, lane : lane + LANES] = tile

    valid_col = (col >= 3) & (col < LANES - 3)
    valid_row = (row >= 3) & (row < LANES - 3)
    target_pair = jnp.where(col < SIDE, col + (LANES - 3), col + (LANES - 3 - SIDE))
    upper = turned_row >= SIDE
    mixed = jnp.where(upper, turned_row, turned_row + SIDE)
    mixed_same = upper == (col < SIDE)
    source_side = jnp.where(upper, turned_row + (LANES - SIDE), turned_row + LANES)
    out_main = (turned_col >= HALO) & (turned_col < LANES - HALO)
    out_second = (turned_col >= SIDE - HALO) & (turned_col < LANES - HALO)
    target_side = jnp.where(
        out_second, turned_col + SIDE, jnp.where(turned_col < SIDE, turned_col + LANES, turned_col)
    )
    source_pair = jnp.where(row < SIDE, row + (LANES - 3), row + (LANES - 3 - SIDE))
    back_same = (row < SIDE) != out_second
    near = jnp.where(valid_row & out_main, jnp.abs(row - turned_col), far)
    cross = jnp.where(valid_row, jnp.abs(row - target_side), far)
    for s, weights in enumerate((FINE, COARSE)):
        lane, start = s * LANES, s * 3 * LANES
        put(main_ref, 0, lane, jnp.where(valid_col, jnp.abs(turned_row - col), far), weights)
        put(side_ref, 0, lane, jnp.where(mixed_same, jnp.abs(mixed - target_pair), far), weights)
        put(side_ref, 3 * LANES, lane, jnp.where(mixed_same, far, jnp.abs(source_side - target_pair)), weights)
        put(back_a_ref, start, 0, near, weights)
        put(back_a_ref, start, LANES, jnp.where(out_second, far, cross), weights)
        put(back_b_ref, start, 0, near, weights)
        put(back_b_ref, start, LANES, jnp.where(out_second, cross, far), weights)
        put(back_s_ref, start, 0, jnp.where(back_same, jnp.abs(source_pair - target_side), far), weights)


def thirds(x):
    high = x.astype(jnp.bfloat16)
    rest = x - high.astype(jnp.float32)
    middle = rest.astype(jnp.bfloat16)
    low = (rest - middle.astype(jnp.float32)).astype(jnp.bfloat16)
    return [high, middle, low]


def times(parts, matrix):
    return jnp.dot(jnp.concatenate(parts, axis=1), matrix, preferred_element_type=jnp.float32)


def fine_taps(ref, i):
    at = lambda d: ref[i, PAD + d : PAD + d + ROWS, :]
    middle = at(0)
    return (at(-1) + at(1)) + (middle + middle)


def coarse_taps(ref, i):
    at = lambda d: ref[i, PAD + d : PAD + d + ROWS, :]
    return (at(-3) + at(3)) + (at(-2) + at(2)) * COARSE[2] + (at(-1) + at(1)) * COARSE[1] + at(0) * COARSE[0]


def mirror(ref, i):
    end = PAD + ROWS
    for outside, inside in ((PAD - 2, PAD), (PAD - 3, PAD + 1), (end + 1, end - 1), (end + 2, end - 2)):
        ref[i, outside : outside + 1, :] = -ref[i, inside : inside + 1, :]


def slope(d, floor):
    return d * lax.rsqrt(d * d + floor)


def work_kernel(
    ens_ref, lat_ref, factor_ref, weight_ref, got_ref, obs_ref, main_ref, side_ref, back_a_ref, back_b_ref, back_s_ref,
    out_ref, fine_ref, coarse_ref, gfine_ref, gcoarse_ref, rows_ref,
):
    me = lat_ref[0]
    factor = factor_ref[2 * ens_ref[0] + (me >> 3)]
    offset = BLOCK * (me & (BLOCKS - 1)) + LANES - HALO
    turned = (lane_ids((ROWS, LANES)) - offset) & (LANES - 1)
    upper = turned >= SIDE
    zeros = jnp.zeros((PAD, LANES), jnp.float32)

    def clear(i, carry):
        for ref in (gfine_ref, gcoarse_ref):
            ref[i, 0:PAD, :] = zeros
            ref[i, PAD + ROWS : 2 * PAD + ROWS, :] = zeros
        return carry

    lax.fori_loop(0, 3 * PAIRS, clear, 0)
    for i in range(rows_ref.shape[0]):
        rows_ref[i, 0:PAD, :] = zeros
        rows_ref[i, PAD + ROWS : 2 * PAD + ROWS, :] = zeros

    def keep(i, slot, both):
        rows_ref[slot, PAD : PAD + ROWS, :] = both[:, :LANES]
        fine_ref[i] = fine_taps(rows_ref, slot)
        rows_ref[slot + 1, PAD : PAD + ROWS, :] = both[:, LANES:]
        mirror(rows_ref, slot + 1)
        coarse_ref[i] = coarse_taps(rows_ref, slot + 1)

    def mix(a, b):
        return jnp.where(upper, a, pltpu.roll(b, SIDE, 1))

    def stack(values):
        return [jnp.concatenate(part, axis=0) for part in zip(*values)]

    def forward(n, carry):
        main, side = [], []
        for q in range(TURN):
            p = TURN * n + q
            a, b, s = (got_ref[p, :, t].reshape(ROWS, LANES) for t in range(3))
            main += [thirds(a), thirds(b)]
            side += [thirds(mix(a, b)) + thirds(s)]
        main = times(stack(main), main_ref[...])
        side = times(stack(side), side_ref[...])
        for q in range(TURN):
            p = TURN * n + q
            for t in range(2):
                r = (2 * q + t) * ROWS
                keep(3 * p + t, 2 * (3 * q + t), main[r : r + ROWS])
            keep(3 * p + 2, 2 * (3 * q + 2), side[q * ROWS : (q + 1) * ROWS])
        return carry

    lax.fori_loop(0, PAIRS // TURN, forward, 0)
    a, s = (jnp.concatenate([obs_ref[me ^ l, t] for l in range(LATS)], axis=0) for t in range(2))
    keep(3 * PAIRS, 0, times(thirds(a), main_ref[...]))
    keep(3 * PAIRS + 1, 2, times(thirds(mix(a, a)) + thirds(s), side_ref[...]))

    def pull_rows(start):
        here, there = pl.ds(start, RC), pl.ds(start + PAD, RC)
        row_weight = jnp.broadcast_to(weight_ref[here, :] * factor, (RC, LANES))
        for ref, gref, scale in ((fine_ref, gfine_ref, FINE_SCALE), (coarse_ref, gcoarse_ref, COARSE_SCALE)):
            floor = 0.01 * scale * scale
            weight = row_weight * (1.0 / scale)
            shared = weight * SHARE
            mains = [3 * (m // 2) + m % 2 for m in range(MEMBERS)]
            value = [ref[i, here, :] for i in mains]
            total = [None] * MEMBERS
            for m in range(MEMBERS):
                for k in range(m + 1, MEMBERS):
                    part = slope(value[m] - value[k], floor)
                    total[m] = part if total[m] is None else total[m] + part
                    total[k] = -part if total[k] is None else total[k] - part
            target = ref[3 * PAIRS, here, :]
            for m, i in enumerate(mains):
                gref[i, there, :] = weight * slope(value[m] - target, floor) - shared * total[m]

            value = [ref[3 * p + 2, here, :] for p in range(PAIRS)]
            other = [pltpu.roll(v, SIDE, 1) for v in value]
            total = [slope(value[p] - other[p], floor) for p in range(PAIRS)]
            swapped = [None] * PAIRS
            for p in range(PAIRS):
                for k in range(p + 1, PAIRS):
                    part = slope(value[p] - value[k], floor)
                    cross = slope(value[p] - other[k], floor)
                    total[p] = total[p] + (part + cross)
                    total[k] = total[k] - part
                    swapped[k] = -cross if swapped[k] is None else swapped[k] - cross
            target = ref[3 * PAIRS + 1, here, :]
            for p in range(PAIRS):
                full = total[p] if swapped[p] is None else total[p] + pltpu.roll(swapped[p], SIDE, 1)
                gref[3 * p + 2, there, :] = weight * slope(value[p] - target, floor) - shared * full

    def pull(n, carry):
        for u in range(UNROLL):
            pull_rows(pl.multiple_of(n * (UNROLL * RC) + u * RC, RC))
        return carry

    lax.fori_loop(0, ROWS // RC // UNROLL, pull, 0)

    def backward(n, carry):
        def parts(i):
            mirror(gcoarse_ref, i)
            return thirds(fine_taps(gfine_ref, i)) + thirds(coarse_taps(gcoarse_ref, i))

        pairs = [TURN * n + q for q in range(TURN)]
        first = times(stack([parts(3 * p) for p in pairs]), back_a_ref[...])
        second = times(stack([parts(3 * p + 1) for p in pairs]), back_b_ref[...])
        side = times(stack([parts(3 * p + 2) for p in pairs]), back_s_ref[...])
        side = side + first[:, LANES:] + second[:, LANES:]
        blocks = (ROWS // RC, RC, LANES)
        for q, p in enumerate(pairs):
            r = slice(q * ROWS, (q + 1) * ROWS)
            out_ref[p, :, 0] = first[r, :LANES].reshape(blocks)
            out_ref[p, :, 1] = second[r, :LANES].reshape(blocks)
            out_ref[p, :, 2] = side[r].reshape(blocks)
        return carry

    lax.fori_loop(0, PAIRS // TURN, backward, 0)


def shape(*dims, dtype=jnp.float32):
    return jax.ShapeDtypeStruct(dims, dtype)


def grant(mib):
    return pltpu.CompilerParams(vmem_limit_bytes=mib << 20)


def exchange_slots(slots):
    slots = slots.reshape(LATS // 2, 2, *slots.shape[1:])
    other = lax.ppermute(slots[:, 1], "lat", [(i, i ^ 1) for i in range(LATS)])
    slots = jnp.stack([slots[:, 0], other], axis=1)
    got = [slots[0]]
    for k in range(1, LATS // 2):
        got.append(lax.ppermute(slots[k], "lat", [(i, i ^ (2 * k)) for i in range(LATS)]))
    return jnp.concatenate(got, axis=0)


def body(prediction_array, verifying_analysis, variable_penalty_factor):
    ens = lax.axis_index("ens").astype(jnp.int32).reshape(1)
    lat = lax.axis_index("lat").astype(jnp.int32).reshape(1)
    degrees = 0.25 * (np.arange(ROWS, dtype=np.float32) - (ROWS - 1) / 2.0)
    lat_weight = jnp.asarray(np.cos(np.deg2rad(degrees)).astype(np.float32)[:, None])

    msg = pl.pallas_call(
        pack_kernel,
        out_shape=shape(128, 3, RC, LANES),
        grid=(PACK,),
        in_specs=[pl.BlockSpec((2, CHANNELS // PACK, RC, COLS), lambda g: (0, g, 0, 0))],
        out_specs=pl.BlockSpec((128 // PACK, 3, RC, LANES), lambda g: (g, 0, 0, 0)),
        compiler_params=grant(8),
        name="pack",
    )(prediction_array)
    got = lax.all_to_all(msg, ("ens", "lat"), 0, 0, tiled=True)
    obs_msg = pl.pallas_call(
        pack_obs_kernel,
        out_shape=shape(LATS, 2, RC, LANES),
        in_specs=[SMEM, VMEM],
        out_specs=VMEM,
        compiler_params=grant(2),
        name="pack_obs",
    )(lat, verifying_analysis)
    obs_got = exchange_slots(obs_msg)
    bf = jnp.bfloat16
    matrices = pl.pallas_call(
        matrices_kernel,
        out_shape=(
            shape(3 * LANES, 2 * LANES, dtype=bf),
            shape(6 * LANES, 2 * LANES, dtype=bf),
            shape(6 * LANES, 2 * LANES, dtype=bf),
            shape(6 * LANES, 2 * LANES, dtype=bf),
            shape(6 * LANES, LANES, dtype=bf),
        ),
        in_specs=[SMEM],
        out_specs=(VMEM,) * 5,
        compiler_params=grant(4),
        cost_estimate=pl.CostEstimate(flops=5_000_000, bytes_accessed=2_000_000, transcendentals=0),
        name="matrices",
    )(lat)
    padded = (ROWS + 2 * PAD, LANES)
    back = pl.pallas_call(
        work_kernel,
        out_shape=shape(PAIRS, ROWS // RC, 3, RC, LANES),
        in_specs=[SMEM] * 3 + [VMEM] * 8,
        out_specs=VMEM,
        scratch_shapes=[
            pltpu.VMEM((3 * PAIRS + 2, ROWS, LANES), jnp.float32),
            pltpu.VMEM((3 * PAIRS + 2, ROWS, LANES), jnp.float32),
            pltpu.VMEM((3 * PAIRS, *padded), jnp.float32),
            pltpu.VMEM((3 * PAIRS, *padded), jnp.float32),
            pltpu.VMEM((6 * TURN, *padded), jnp.float32),
        ],
        compiler_params=grant(16),
        name="work",
    )(ens, lat, variable_penalty_factor, lat_weight, got.reshape(PAIRS, ROWS // RC, 3, RC, LANES), obs_got, *matrices)
    ret = lax.all_to_all(back.reshape(128, 3, RC, LANES), ("ens", "lat"), 0, 0, tiled=True)
    return pl.pallas_call(
        unpack_kernel,
        out_shape=shape(2, CHANNELS, RC, COLS),
        in_specs=[VMEM],
        out_specs=VMEM,
        compiler_params=grant(8),
        name="unpack",
    )(ret)


def solution(mesh):
    placed = (P("ens", None, "lat", None), P("ens", "lat", None), P())
    return jax.shard_map(
        body, mesh=mesh, in_specs=placed, out_specs=P("ens", None, "lat", None), check_vma=False
    )
```

```python
import jax
import jax.numpy as jnp
import numpy as np
from jax import lax
from jax.experimental import pallas as pl
from jax.experimental.pallas import tpu as pltpu
from jax.sharding import PartitionSpec as P

MEMBERS, CHANNELS, ROWS, COLS = 16, 16, 128, 1440
BLOCKS = 8
BLOCK = COLS // BLOCKS
LANES, SIDE, HALO = 128, 64, 6
PAIRS = MEMBERS // 2
RC = 8
PAD = 8
LATS = 16
SHARE = 0.95 / (MEMBERS - 1)
FINE, COARSE = (2, 1), (20, 15, 6, 1)
FINE_SCALE, COARSE_SCALE = 16.0, 4096.0
TURN, UNROLL = 4, 4
PACK = 8
VMEM = pl.BlockSpec(memory_space=pltpu.VMEM)
HBM = pl.BlockSpec(memory_space=pltpu.HBM)
SMEM = pl.BlockSpec(memory_space=pltpu.SMEM)


def offset_of(block):
    return (BLOCK * block + LANES - HALO) % LANES


def lane_ids(shape=(RC, LANES)):
    return lax.broadcasted_iota(jnp.int32, shape, len(shape) - 1)


def column_runs(wanted):
    runs = []
    for lane, col in wanted:
        if runs:
            p, q, n = runs[-1]
            if p + n == lane and q + n == col and col % LANES:
                runs[-1] = (p, q, n + 1)
                continue
        runs.append((lane, col, 1))
    return runs


def gather_tile(load, parts, lanes):
    tile = None
    for source, p, q, n in parts:
        base = min(q // LANES * LANES, COLS - LANES)
        piece = load(source, base)
        shift = (p - (q - base)) % LANES
        if shift:
            piece = pltpu.roll(piece, shift, 1)
        tile = piece if tile is None else jnp.where((lanes >= p) & (lanes < p + n), piece, tile)
    return tile


def main_parts(source, block):
    o = offset_of(block)
    lanes = sorted(range(LANES), key=lambda j: (j + o) % LANES)
    runs = column_runs([((j + o) % LANES, (BLOCK * block - HALO + j) % COLS) for j in lanes])
    return [(source, p, q, n) for p, q, n in runs]


def side_parts(first, second, block):
    o = offset_of(block)
    parts = []
    for source, half in ((first, 0), (second, 1)):
        wanted = [
            ((r + o) % LANES, (BLOCK * block - HALO + LANES + r % SIDE) % COLS)
            for r in range(half * SIDE, (half + 1) * SIDE)
        ]
        parts += [(source, p, q, n) for p, q, n in column_runs(sorted(wanted))]
    return parts


def pack_obs_kernel(lat_ref, obs_ref, obs_msg_ref):
    lanes = lane_ids()
    me = lat_ref[0]

    def load_obs(source, base):
        return obs_ref[source, :, base : base + LANES]

    for h in range(2):
        for b in range(BLOCKS):
            slot = me ^ (h * BLOCKS + b)
            obs_msg_ref[slot, 0] = gather_tile(load_obs, main_parts(h, b), lanes)
            obs_msg_ref[slot, 1] = gather_tile(load_obs, side_parts(h, h, b), lanes)


def pack_kernel(x_ref, msg_ref, x_buf, msg_buf, in_sem, out_sem):
    lanes = lane_ids()
    per = CHANNELS // PACK

    def fetch(g):
        return pltpu.make_async_copy(x_ref.at[:, g * per : (g + 1) * per], x_buf.at[g], in_sem.at[g])

    def push(g):
        rows = per * BLOCKS
        return pltpu.make_async_copy(msg_buf.at[g], msg_ref.at[g * rows : (g + 1) * rows], out_sem.at[g])

    for g in range(PACK):
        fetch(g).start()
    for g in range(PACK):
        fetch(g).wait()
        for c in range(per):
            def load(source, base):
                return x_buf[g, source, c, :, base : base + LANES]

            for b in range(BLOCKS):
                dst = c * BLOCKS + b
                msg_buf[g, dst, 0] = gather_tile(load, main_parts(0, b), lanes)
                msg_buf[g, dst, 1] = gather_tile(load, main_parts(1, b), lanes)
                msg_buf[g, dst, 2] = gather_tile(load, side_parts(0, 1, b), lanes)
        push(g).start()
    for g in range(PACK):
        push(g).wait()


def unpack_kernel(ret_ref, out_ref, out_buf, out_sem):
    lanes = lane_ids()
    per = CHANNELS // PACK

    def push(g):
        return pltpu.make_async_copy(out_buf.at[g], out_ref.at[:, g * per : (g + 1) * per], out_sem.at[g])

    for g in range(PACK):
        for c in range(per):
            for m in range(2):
                for t in range((COLS + LANES - 1) // LANES):
                    tile = None
                    q = t * LANES
                    end = min(q + LANES, COLS)
                    while q < end:
                        b, k = q // BLOCK, q % BLOCK
                        stop = b * BLOCK + (BLOCK - SIDE if k < BLOCK - SIDE else BLOCK)
                        src = (g * per + c) * BLOCKS + b
                        if k < BLOCK - SIDE:
                            piece = ret_ref[src, m]
                        else:
                            piece = ret_ref[src, 2]
                            if m:
                                piece = pltpu.roll(piece, SIDE, 1)
                        p = q - t * LANES
                        tile = piece if tile is None else jnp.where(lanes >= p, piece, tile)
                        q = min(stop, end)
                    if end - t * LANES == LANES:
                        out_buf[g, m, c, :, t * LANES : end] = tile
                    else:
                        out_buf[g, m, c, :, t * LANES : end] = tile[:, : end - t * LANES]
        push(g).start()
    for g in range(PACK):
        push(g).wait()


def taps(distance, weights):
    value = jnp.zeros(distance.shape, jnp.float32)
    for d, w in enumerate(weights):
        value = jnp.where(distance == d, w, value)
    return value


def matrices_kernel(lat_ref, main_ref, side_ref, back_a_ref, back_b_ref, back_s_ref):
    offset = BLOCK * (lat_ref[0] & (BLOCKS - 1)) + LANES - HALO
    size = (LANES, LANES)
    row = lax.broadcasted_iota(jnp.int32, size, 0)
    col = lax.broadcasted_iota(jnp.int32, size, 1)
    turned_row = (row - offset) & (LANES - 1)
    turned_col = (col - offset) & (LANES - 1)
    far = 99

    def put(ref, start, lane, distance, weights):
        tile = taps(distance, weights).astype(jnp.bfloat16)
        for i in range(3):
            ref[start + i * LANES : start + (i + 1) * LANES, lane : lane + LANES] = tile

    valid_col = (col >= 3) & (col < LANES - 3)
    valid_row = (row >= 3) & (row < LANES - 3)
    target_pair = jnp.where(col < SIDE, col + (LANES - 3), col + (LANES - 3 - SIDE))
    upper = turned_row >= SIDE
    mixed = jnp.where(upper, turned_row, turned_row + SIDE)
    mixed_same = upper == (col < SIDE)
    source_side = jnp.where(upper, turned_row + (LANES - SIDE), turned_row + LANES)
    out_main = (turned_col >= HALO) & (turned_col < LANES - HALO)
    out_second = (turned_col >= SIDE - HALO) & (turned_col < LANES - HALO)
    target_side = jnp.where(
        out_second, turned_col + SIDE, jnp.where(turned_col < SIDE, turned_col + LANES, turned_col)
    )
    source_pair = jnp.where(row < SIDE, row + (LANES - 3), row + (LANES - 3 - SIDE))
    back_same = (row < SIDE) != out_second
    near = jnp.where(valid_row & out_main, jnp.abs(row - turned_col), far)
    cross = jnp.where(valid_row, jnp.abs(row - target_side), far)
    for s, weights in enumerate((FINE, COARSE)):
        lane, start = s * LANES, s * 3 * LANES
        put(main_ref, 0, lane, jnp.where(valid_col, jnp.abs(turned_row - col), far), weights)
        put(side_ref, 0, lane, jnp.where(mixed_same, jnp.abs(mixed - target_pair), far), weights)
        put(side_ref, 3 * LANES, lane, jnp.where(mixed_same, far, jnp.abs(source_side - target_pair)), weights)
        put(back_a_ref, start, 0, near, weights)
        put(back_a_ref, start, LANES, jnp.where(out_second, far, cross), weights)
        put(back_b_ref, start, 0, near, weights)
        put(back_b_ref, start, LANES, jnp.where(out_second, cross, far), weights)
        put(back_s_ref, start, 0, jnp.where(back_same, jnp.abs(source_pair - target_side), far), weights)


def thirds(x):
    high = x.astype(jnp.bfloat16)
    rest = x - high.astype(jnp.float32)
    middle = rest.astype(jnp.bfloat16)
    low = (rest - middle.astype(jnp.float32)).astype(jnp.bfloat16)
    return [high, middle, low]


def times(parts, matrix):
    return jnp.dot(jnp.concatenate(parts, axis=1), matrix, preferred_element_type=jnp.float32)


def fine_taps(ref, i):
    at = lambda d: ref[i, PAD + d : PAD + d + ROWS, :]
    middle = at(0)
    return (at(-1) + at(1)) + (middle + middle)


def coarse_taps(ref, i):
    at = lambda d: ref[i, PAD + d : PAD + d + ROWS, :]
    return (at(-3) + at(3)) + (at(-2) + at(2)) * COARSE[2] + (at(-1) + at(1)) * COARSE[1] + at(0) * COARSE[0]


def mirror(ref, i):
    end = PAD + ROWS
    for outside, inside in ((PAD - 2, PAD), (PAD - 3, PAD + 1), (end + 1, end - 1), (end + 2, end - 2)):
        ref[i, outside : outside + 1, :] = -ref[i, inside : inside + 1, :]


def slope(d, floor):
    return d * lax.rsqrt(d * d + floor)


def work_kernel(
    ens_ref, lat_ref, factor_ref, weight_ref, got_ref, obs_ref, main_ref, side_ref, back_a_ref, back_b_ref, back_s_ref,
    out_ref, fine_ref, coarse_ref, gfine_ref, gcoarse_ref, rows_ref,
):
    me = lat_ref[0]
    factor = factor_ref[2 * ens_ref[0] + (me >> 3)]
    offset = BLOCK * (me & (BLOCKS - 1)) + LANES - HALO
    turned = (lane_ids((ROWS, LANES)) - offset) & (LANES - 1)
    upper = turned >= SIDE
    zeros = jnp.zeros((PAD, LANES), jnp.float32)

    def clear(i, carry):
        for ref in (gfine_ref, gcoarse_ref):
            ref[i, 0:PAD, :] = zeros
            ref[i, PAD + ROWS : 2 * PAD + ROWS, :] = zeros
        return carry

    lax.fori_loop(0, 3 * PAIRS, clear, 0)
    for i in range(rows_ref.shape[0]):
        rows_ref[i, 0:PAD, :] = zeros
        rows_ref[i, PAD + ROWS : 2 * PAD + ROWS, :] = zeros

    def keep(i, slot, both):
        rows_ref[slot, PAD : PAD + ROWS, :] = both[:, :LANES]
        fine_ref[i] = fine_taps(rows_ref, slot)
        rows_ref[slot + 1, PAD : PAD + ROWS, :] = both[:, LANES:]
        mirror(rows_ref, slot + 1)
        coarse_ref[i] = coarse_taps(rows_ref, slot + 1)

    def mix(a, b):
        return jnp.where(upper, a, pltpu.roll(b, SIDE, 1))

    def stack(values):
        return [jnp.concatenate(part, axis=0) for part in zip(*values)]

    def forward(n, carry):
        main, side = [], []
        for q in range(TURN):
            p = TURN * n + q
            a, b, s = (got_ref[p, :, t].reshape(ROWS, LANES) for t in range(3))
            main += [thirds(a), thirds(b)]
            side += [thirds(mix(a, b)) + thirds(s)]
        main = times(stack(main), main_ref[...])
        side = times(stack(side), side_ref[...])
        for q in range(TURN):
            p = TURN * n + q
            for t in range(2):
                r = (2 * q + t) * ROWS
                keep(3 * p + t, 2 * (3 * q + t), main[r : r + ROWS])
            keep(3 * p + 2, 2 * (3 * q + 2), side[q * ROWS : (q + 1) * ROWS])
        return carry

    lax.fori_loop(0, PAIRS // TURN, forward, 0)
    a, s = (jnp.concatenate([obs_ref[me ^ l, t] for l in range(LATS)], axis=0) for t in range(2))
    keep(3 * PAIRS, 0, times(thirds(a), main_ref[...]))
    keep(3 * PAIRS + 1, 2, times(thirds(mix(a, a)) + thirds(s), side_ref[...]))

    def pull_rows(start):
        here, there = pl.ds(start, RC), pl.ds(start + PAD, RC)
        row_weight = jnp.broadcast_to(weight_ref[here, :] * factor, (RC, LANES))
        for ref, gref, scale in ((fine_ref, gfine_ref, FINE_SCALE), (coarse_ref, gcoarse_ref, COARSE_SCALE)):
            floor = 0.01 * scale * scale
            weight = row_weight * (1.0 / scale)
            shared = weight * SHARE
            mains = [3 * (m // 2) + m % 2 for m in range(MEMBERS)]
            value = [ref[i, here, :] for i in mains]
            total = [None] * MEMBERS
            for m in range(MEMBERS):
                for k in range(m + 1, MEMBERS):
                    part = slope(value[m] - value[k], floor)
                    total[m] = part if total[m] is None else total[m] + part
                    total[k] = -part if total[k] is None else total[k] - part
            target = ref[3 * PAIRS, here, :]
            for m, i in enumerate(mains):
                gref[i, there, :] = weight * slope(value[m] - target, floor) - shared * total[m]

            value = [ref[3 * p + 2, here, :] for p in range(PAIRS)]
            other = [pltpu.roll(v, SIDE, 1) for v in value]
            total = [slope(value[p] - other[p], floor) for p in range(PAIRS)]
            swapped = [None] * PAIRS
            for p in range(PAIRS):
                for k in range(p + 1, PAIRS):
                    part = slope(value[p] - value[k], floor)
                    cross = slope(value[p] - other[k], floor)
                    total[p] = total[p] + (part + cross)
                    total[k] = total[k] - part
                    swapped[k] = -cross if swapped[k] is None else swapped[k] - cross
            target = ref[3 * PAIRS + 1, here, :]
            for p in range(PAIRS):
                full = total[p] if swapped[p] is None else total[p] + pltpu.roll(swapped[p], SIDE, 1)
                gref[3 * p + 2, there, :] = weight * slope(value[p] - target, floor) - shared * full

    def pull(n, carry):
        for u in range(UNROLL):
            pull_rows(pl.multiple_of(n * (UNROLL * RC) + u * RC, RC))
        return carry

    lax.fori_loop(0, ROWS // RC // UNROLL, pull, 0)

    def backward(n, carry):
        def parts(i):
            mirror(gcoarse_ref, i)
            return thirds(fine_taps(gfine_ref, i)) + thirds(coarse_taps(gcoarse_ref, i))

        pairs = [TURN * n + q for q in range(TURN)]
        first = times(stack([parts(3 * p) for p in pairs]), back_a_ref[...])
        second = times(stack([parts(3 * p + 1) for p in pairs]), back_b_ref[...])
        side = times(stack([parts(3 * p + 2) for p in pairs]), back_s_ref[...])
        side = side + first[:, LANES:] + second[:, LANES:]
        blocks = (ROWS // RC, RC, LANES)
        for q, p in enumerate(pairs):
            r = slice(q * ROWS, (q + 1) * ROWS)
            out_ref[p, :, 0] = first[r, :LANES].reshape(blocks)
            out_ref[p, :, 1] = second[r, :LANES].reshape(blocks)
            out_ref[p, :, 2] = side[r].reshape(blocks)
        return carry

    lax.fori_loop(0, PAIRS // TURN, backward, 0)


def shape(*dims, dtype=jnp.float32):
    return jax.ShapeDtypeStruct(dims, dtype)


def grant(mib):
    return pltpu.CompilerParams(vmem_limit_bytes=mib << 20)


def exchange_slots(slots):
    slots = slots.reshape(LATS // 2, 2, *slots.shape[1:])
    other = lax.ppermute(slots[:, 1], "lat", [(i, i ^ 1) for i in range(LATS)])
    slots = jnp.stack([slots[:, 0], other], axis=1)
    got = [slots[0]]
    for k in range(1, LATS // 2):
        got.append(lax.ppermute(slots[k], "lat", [(i, i ^ (2 * k)) for i in range(LATS)]))
    return jnp.concatenate(got, axis=0)


def body(prediction_array, verifying_analysis, variable_penalty_factor):
    ens = lax.axis_index("ens").astype(jnp.int32).reshape(1)
    lat = lax.axis_index("lat").astype(jnp.int32).reshape(1)
    degrees = 0.25 * (np.arange(ROWS, dtype=np.float32) - (ROWS - 1) / 2.0)
    lat_weight = jnp.asarray(np.cos(np.deg2rad(degrees)).astype(np.float32)[:, None])

    msg = pl.pallas_call(
        pack_kernel,
        out_shape=shape(128, 3, RC, LANES),
        in_specs=[HBM],
        out_specs=HBM,
        scratch_shapes=[
            pltpu.VMEM((PACK, 2, CHANNELS // PACK, RC, COLS), jnp.float32),
            pltpu.VMEM((PACK, 128 // PACK, 3, RC, LANES), jnp.float32),
            pltpu.SemaphoreType.DMA((PACK,)),
            pltpu.SemaphoreType.DMA((PACK,)),
        ],
        compiler_params=grant(60),
        name="pack",
    )(prediction_array)
    got = lax.all_to_all(msg, ("ens", "lat"), 0, 0, tiled=True)
    obs_msg = pl.pallas_call(
        pack_obs_kernel,
        out_shape=shape(LATS, 2, RC, LANES),
        in_specs=[SMEM, VMEM],
        out_specs=VMEM,
        compiler_params=grant(2),
        name="pack_obs",
    )(lat, verifying_analysis)
    obs_got = exchange_slots(obs_msg)
    bf = jnp.bfloat16
    matrices = pl.pallas_call(
        matrices_kernel,
        out_shape=(
            shape(3 * LANES, 2 * LANES, dtype=bf),
            shape(6 * LANES, 2 * LANES, dtype=bf),
            shape(6 * LANES, 2 * LANES, dtype=bf),
            shape(6 * LANES, 2 * LANES, dtype=bf),
            shape(6 * LANES, LANES, dtype=bf),
        ),
        in_specs=[SMEM],
        out_specs=(VMEM,) * 5,
        compiler_params=grant(4),
        cost_estimate=pl.CostEstimate(flops=5_000_000, bytes_accessed=2_000_000, transcendentals=0),
        name="matrices",
    )(lat)
    padded = (ROWS + 2 * PAD, LANES)
    back = pl.pallas_call(
        work_kernel,
        out_shape=shape(PAIRS, ROWS // RC, 3, RC, LANES),
        in_specs=[SMEM] * 3 + [VMEM] * 8,
        out_specs=VMEM,
        scratch_shapes=[
            pltpu.VMEM((3 * PAIRS + 2, ROWS, LANES), jnp.float32),
            pltpu.VMEM((3 * PAIRS + 2, ROWS, LANES), jnp.float32),
            pltpu.VMEM((3 * PAIRS, *padded), jnp.float32),
            pltpu.VMEM((3 * PAIRS, *padded), jnp.float32),
            pltpu.VMEM((6 * TURN, *padded), jnp.float32),
        ],
        compiler_params=grant(16),
        name="work",
    )(ens, lat, variable_penalty_factor, lat_weight, got.reshape(PAIRS, ROWS // RC, 3, RC, LANES), obs_got, *matrices)
    ret = lax.all_to_all(back.reshape(128, 3, RC, LANES), ("ens", "lat"), 0, 0, tiled=True)
    return pl.pallas_call(
        unpack_kernel,
        out_shape=shape(2, CHANNELS, RC, COLS),
        in_specs=[VMEM],
        out_specs=HBM,
        scratch_shapes=[
            pltpu.VMEM((PACK, 2, CHANNELS // PACK, RC, COLS), jnp.float32),
            pltpu.SemaphoreType.DMA((PACK,)),
        ],
        compiler_params=grant(8),
        name="unpack",
    )(ret)


def solution(mesh):
    placed = (P("ens", None, "lat", None), P("ens", "lat", None), P())
    return jax.shard_map(
        body, mesh=mesh, in_specs=placed, out_specs=P("ens", None, "lat", None), check_vma=False
    )
```

```python
import jax
import jax.numpy as jnp
import numpy as np
from jax import lax
from jax.experimental import pallas as pl
from jax.experimental.pallas import tpu as pltpu
from jax.sharding import PartitionSpec as P

MEMBERS, CHANNELS, ROWS, COLS = 16, 16, 128, 1440
BLOCKS = 8
BLOCK = COLS // BLOCKS
LANES, SIDE, HALO = 128, 64, 6
PAIRS = MEMBERS // 2
RC = 8
PAD = 8
LATS = 16
SHARE = 0.95 / (MEMBERS - 1)
FINE, COARSE = (2, 1), (20, 15, 6, 1)
FINE_SCALE, COARSE_SCALE = 16.0, 4096.0
TURN, UNROLL = 4, 4
PACK = 4
VMEM = pl.BlockSpec(memory_space=pltpu.VMEM)
HBM = pl.BlockSpec(memory_space=pltpu.HBM)
SMEM = pl.BlockSpec(memory_space=pltpu.SMEM)


def offset_of(block):
    return (BLOCK * block + LANES - HALO) % LANES


def lane_ids(shape=(RC, LANES)):
    return lax.broadcasted_iota(jnp.int32, shape, len(shape) - 1)


def column_runs(wanted):
    runs = []
    for lane, col in wanted:
        if runs:
            p, q, n = runs[-1]
            if p + n == lane and q + n == col and col % LANES:
                runs[-1] = (p, q, n + 1)
                continue
        runs.append((lane, col, 1))
    return runs


def gather_tile(load, parts, lanes):
    tile = None
    for source, p, q, n in parts:
        base = min(q // LANES * LANES, COLS - LANES)
        piece = load(source, base)
        shift = (p - (q - base)) % LANES
        if shift:
            piece = pltpu.roll(piece, shift, 1)
        tile = piece if tile is None else jnp.where((lanes >= p) & (lanes < p + n), piece, tile)
    return tile


def main_parts(source, block):
    o = offset_of(block)
    lanes = sorted(range(LANES), key=lambda j: (j + o) % LANES)
    runs = column_runs([((j + o) % LANES, (BLOCK * block - HALO + j) % COLS) for j in lanes])
    return [(source, p, q, n) for p, q, n in runs]


def side_parts(first, second, block):
    o = offset_of(block)
    parts = []
    for source, half in ((first, 0), (second, 1)):
        wanted = [
            ((r + o) % LANES, (BLOCK * block - HALO + LANES + r % SIDE) % COLS)
            for r in range(half * SIDE, (half + 1) * SIDE)
        ]
        parts += [(source, p, q, n) for p, q, n in column_runs(sorted(wanted))]
    return parts


def pack_obs_kernel(lat_ref, obs_ref, obs_msg_ref):
    lanes = lane_ids()
    me = lat_ref[0]

    def load_obs(source, base):
        return obs_ref[source, :, base : base + LANES]

    for h in range(2):
        for b in range(BLOCKS):
            slot = me ^ (h * BLOCKS + b)
            obs_msg_ref[slot, 0] = gather_tile(load_obs, main_parts(h, b), lanes)
            obs_msg_ref[slot, 1] = gather_tile(load_obs, side_parts(h, h, b), lanes)


def pack_kernel(x_ref, msg_ref, x_buf, msg_buf, in_sem, out_sem):
    lanes = lane_ids()
    per = CHANNELS // PACK

    def fetch(g):
        return pltpu.make_async_copy(x_ref.at[:, g * per : (g + 1) * per], x_buf.at[g], in_sem.at[g])

    def push(g):
        rows = per * BLOCKS
        return pltpu.make_async_copy(msg_buf.at[g], msg_ref.at[g * rows : (g + 1) * rows], out_sem.at[g])

    for g in range(PACK):
        fetch(g).start()
    for g in range(PACK):
        fetch(g).wait()
        for c in range(per):
            def load(source, base):
                return x_buf[g, source, c, :, base : base + LANES]

            for b in range(BLOCKS):
                dst = c * BLOCKS + b
                msg_buf[g, dst, 0] = gather_tile(load, main_parts(0, b), lanes)
                msg_buf[g, dst, 1] = gather_tile(load, main_parts(1, b), lanes)
                msg_buf[g, dst, 2] = gather_tile(load, side_parts(0, 1, b), lanes)
        push(g).start()
    for g in range(PACK):
        push(g).wait()


def unpack_kernel(ret_ref, out_ref, out_buf, out_sem):
    lanes = lane_ids()
    per = CHANNELS // PACK

    def push(g):
        return pltpu.make_async_copy(out_buf.at[g], out_ref.at[:, g * per : (g + 1) * per], out_sem.at[g])

    for g in range(PACK):
        for c in range(per):
            for m in range(2):
                for t in range((COLS + LANES - 1) // LANES):
                    tile = None
                    q = t * LANES
                    end = min(q + LANES, COLS)
                    while q < end:
                        b, k = q // BLOCK, q % BLOCK
                        stop = b * BLOCK + (BLOCK - SIDE if k < BLOCK - SIDE else BLOCK)
                        src = (g * per + c) * BLOCKS + b
                        if k < BLOCK - SIDE:
                            piece = ret_ref[src, m]
                        else:
                            piece = ret_ref[src, 2]
                            if m:
                                piece = pltpu.roll(piece, SIDE, 1)
                        p = q - t * LANES
                        tile = piece if tile is None else jnp.where(lanes >= p, piece, tile)
                        q = min(stop, end)
                    if end - t * LANES == LANES:
                        out_buf[g, m, c, :, t * LANES : end] = tile
                    else:
                        out_buf[g, m, c, :, t * LANES : end] = tile[:, : end - t * LANES]
        push(g).start()
    for g in range(PACK):
        push(g).wait()


def taps(distance, weights):
    value = jnp.zeros(distance.shape, jnp.float32)
    for d, w in enumerate(weights):
        value = jnp.where(distance == d, w, value)
    return value


def matrices_kernel(lat_ref, main_ref, side_ref, back_a_ref, back_b_ref, back_s_ref):
    offset = BLOCK * (lat_ref[0] & (BLOCKS - 1)) + LANES - HALO
    size = (LANES, LANES)
    row = lax.broadcasted_iota(jnp.int32, size, 0)
    col = lax.broadcasted_iota(jnp.int32, size, 1)
    turned_row = (row - offset) & (LANES - 1)
    turned_col = (col - offset) & (LANES - 1)
    far = 99

    def put(ref, start, lane, distance, weights):
        tile = taps(distance, weights).astype(jnp.bfloat16)
        for i in range(3):
            ref[start + i * LANES : start + (i + 1) * LANES, lane : lane + LANES] = tile

    valid_col = (col >= 3) & (col < LANES - 3)
    valid_row = (row >= 3) & (row < LANES - 3)
    target_pair = jnp.where(col < SIDE, col + (LANES - 3), col + (LANES - 3 - SIDE))
    upper = turned_row >= SIDE
    mixed = jnp.where(upper, turned_row, turned_row + SIDE)
    mixed_same = upper == (col < SIDE)
    source_side = jnp.where(upper, turned_row + (LANES - SIDE), turned_row + LANES)
    out_main = (turned_col >= HALO) & (turned_col < LANES - HALO)
    out_second = (turned_col >= SIDE - HALO) & (turned_col < LANES - HALO)
    target_side = jnp.where(
        out_second, turned_col + SIDE, jnp.where(turned_col < SIDE, turned_col + LANES, turned_col)
    )
    source_pair = jnp.where(row < SIDE, row + (LANES - 3), row + (LANES - 3 - SIDE))
    back_same = (row < SIDE) != out_second
    near = jnp.where(valid_row & out_main, jnp.abs(row - turned_col), far)
    cross = jnp.where(valid_row, jnp.abs(row - target_side), far)
    for s, weights in enumerate((FINE, COARSE)):
        lane, start = s * LANES, s * 3 * LANES
        put(main_ref, 0, lane, jnp.where(valid_col, jnp.abs(turned_row - col), far), weights)
        put(side_ref, 0, lane, jnp.where(mixed_same, jnp.abs(mixed - target_pair), far), weights)
        put(side_ref, 3 * LANES, lane, jnp.where(mixed_same, far, jnp.abs(source_side - target_pair)), weights)
        put(back_a_ref, start, 0, near, weights)
        put(back_a_ref, start, LANES, jnp.where(out_second, far, cross), weights)
        put(back_b_ref, start, 0, near, weights)
        put(back_b_ref, start, LANES, jnp.where(out_second, cross, far), weights)
        put(back_s_ref, start, 0, jnp.where(back_same, jnp.abs(source_pair - target_side), far), weights)


def thirds(x):
    high = x.astype(jnp.bfloat16)
    rest = x - high.astype(jnp.float32)
    middle = rest.astype(jnp.bfloat16)
    low = (rest - middle.astype(jnp.float32)).astype(jnp.bfloat16)
    return [high, middle, low]


def times(parts, matrix):
    return jnp.dot(jnp.concatenate(parts, axis=1), matrix, preferred_element_type=jnp.float32)


def fine_taps(ref, i):
    at = lambda d: ref[i, PAD + d : PAD + d + ROWS, :]
    middle = at(0)
    return (at(-1) + at(1)) + (middle + middle)


def coarse_taps(ref, i):
    at = lambda d: ref[i, PAD + d : PAD + d + ROWS, :]
    return (at(-3) + at(3)) + (at(-2) + at(2)) * COARSE[2] + (at(-1) + at(1)) * COARSE[1] + at(0) * COARSE[0]


def mirror(ref, i):
    end = PAD + ROWS
    for outside, inside in ((PAD - 2, PAD), (PAD - 3, PAD + 1), (end + 1, end - 1), (end + 2, end - 2)):
        ref[i, outside : outside + 1, :] = -ref[i, inside : inside + 1, :]


def slope(d, floor):
    return d * lax.rsqrt(d * d + floor)


def work_kernel(
    ens_ref, lat_ref, factor_ref, weight_ref, got_ref, obs_ref, main_ref, side_ref, back_a_ref, back_b_ref, back_s_ref,
    out_ref, fine_ref, coarse_ref, gfine_ref, gcoarse_ref, rows_ref,
):
    me = lat_ref[0]
    factor = factor_ref[2 * ens_ref[0] + (me >> 3)]
    offset = BLOCK * (me & (BLOCKS - 1)) + LANES - HALO
    turned = (lane_ids((ROWS, LANES)) - offset) & (LANES - 1)
    upper = turned >= SIDE
    zeros = jnp.zeros((PAD, LANES), jnp.float32)

    def clear(i, carry):
        for ref in (gfine_ref, gcoarse_ref):
            ref[i, 0:PAD, :] = zeros
            ref[i, PAD + ROWS : 2 * PAD + ROWS, :] = zeros
        return carry

    lax.fori_loop(0, 3 * PAIRS, clear, 0)
    for i in range(rows_ref.shape[0]):
        rows_ref[i, 0:PAD, :] = zeros
        rows_ref[i, PAD + ROWS : 2 * PAD + ROWS, :] = zeros

    def keep(i, slot, both):
        rows_ref[slot, PAD : PAD + ROWS, :] = both[:, :LANES]
        fine_ref[i] = fine_taps(rows_ref, slot)
        rows_ref[slot + 1, PAD : PAD + ROWS, :] = both[:, LANES:]
        mirror(rows_ref, slot + 1)
        coarse_ref[i] = coarse_taps(rows_ref, slot + 1)

    def mix(a, b):
        return jnp.where(upper, a, pltpu.roll(b, SIDE, 1))

    def stack(values):
        return [jnp.concatenate(part, axis=0) for part in zip(*values)]

    def forward(n, carry):
        main, side = [], []
        for q in range(TURN):
            p = TURN * n + q
            a, b, s = (got_ref[p, :, t].reshape(ROWS, LANES) for t in range(3))
            main += [thirds(a), thirds(b)]
            side += [thirds(mix(a, b)) + thirds(s)]
        main = times(stack(main), main_ref[...])
        side = times(stack(side), side_ref[...])
        for q in range(TURN):
            p = TURN * n + q
            for t in range(2):
                r = (2 * q + t) * ROWS
                keep(3 * p + t, 2 * (3 * q + t), main[r : r + ROWS])
            keep(3 * p + 2, 2 * (3 * q + 2), side[q * ROWS : (q + 1) * ROWS])
        return carry

    for n in range(PAIRS // TURN):
        forward(n, 0)
    a, s = (jnp.concatenate([obs_ref[me ^ l, t] for l in range(LATS)], axis=0) for t in range(2))
    keep(3 * PAIRS, 0, times(thirds(a), main_ref[...]))
    keep(3 * PAIRS + 1, 2, times(thirds(mix(a, a)) + thirds(s), side_ref[...]))

    def pull_rows(start):
        here, there = pl.ds(start, RC), pl.ds(start + PAD, RC)
        row_weight = jnp.broadcast_to(weight_ref[here, :] * factor, (RC, LANES))
        for ref, gref, scale in ((fine_ref, gfine_ref, FINE_SCALE), (coarse_ref, gcoarse_ref, COARSE_SCALE)):
            floor = 0.01 * scale * scale
            weight = row_weight * (1.0 / scale)
            shared = weight * SHARE
            mains = [3 * (m // 2) + m % 2 for m in range(MEMBERS)]
            value = [ref[i, here, :] for i in mains]
            total = [None] * MEMBERS
            for m in range(MEMBERS):
                for k in range(m + 1, MEMBERS):
                    part = slope(value[m] - value[k], floor)
                    total[m] = part if total[m] is None else total[m] + part
                    total[k] = -part if total[k] is None else total[k] - part
            target = ref[3 * PAIRS, here, :]
            for m, i in enumerate(mains):
                gref[i, there, :] = weight * slope(value[m] - target, floor) - shared * total[m]

            value = [ref[3 * p + 2, here, :] for p in range(PAIRS)]
            other = [pltpu.roll(v, SIDE, 1) for v in value]
            total = [slope(value[p] - other[p], floor) for p in range(PAIRS)]
            swapped = [None] * PAIRS
            for p in range(PAIRS):
                for k in range(p + 1, PAIRS):
                    part = slope(value[p] - value[k], floor)
                    cross = slope(value[p] - other[k], floor)
                    total[p] = total[p] + (part + cross)
                    total[k] = total[k] - part
                    swapped[k] = -cross if swapped[k] is None else swapped[k] - cross
            target = ref[3 * PAIRS + 1, here, :]
            for p in range(PAIRS):
                full = total[p] if swapped[p] is None else total[p] + pltpu.roll(swapped[p], SIDE, 1)
                gref[3 * p + 2, there, :] = weight * slope(value[p] - target, floor) - shared * full

    def pull(n, carry):
        for u in range(UNROLL):
            pull_rows(pl.multiple_of(n * (UNROLL * RC) + u * RC, RC))
        return carry

    lax.fori_loop(0, ROWS // RC // UNROLL, pull, 0)

    def backward(n, carry):
        def parts(i):
            mirror(gcoarse_ref, i)
            return thirds(fine_taps(gfine_ref, i)) + thirds(coarse_taps(gcoarse_ref, i))

        pairs = [TURN * n + q for q in range(TURN)]
        first = times(stack([parts(3 * p) for p in pairs]), back_a_ref[...])
        second = times(stack([parts(3 * p + 1) for p in pairs]), back_b_ref[...])
        side = times(stack([parts(3 * p + 2) for p in pairs]), back_s_ref[...])
        side = side + first[:, LANES:] + second[:, LANES:]
        blocks = (ROWS // RC, RC, LANES)
        for q, p in enumerate(pairs):
            r = slice(q * ROWS, (q + 1) * ROWS)
            out_ref[p, :, 0] = first[r, :LANES].reshape(blocks)
            out_ref[p, :, 1] = second[r, :LANES].reshape(blocks)
            out_ref[p, :, 2] = side[r].reshape(blocks)
        return carry

    for n in range(PAIRS // TURN):
        backward(n, 0)


def shape(*dims, dtype=jnp.float32):
    return jax.ShapeDtypeStruct(dims, dtype)


def grant(mib):
    return pltpu.CompilerParams(vmem_limit_bytes=mib << 20)


def exchange_slots(slots):
    slots = slots.reshape(LATS // 2, 2, *slots.shape[1:])
    other = lax.ppermute(slots[:, 1], "lat", [(i, i ^ 1) for i in range(LATS)])
    slots = jnp.stack([slots[:, 0], other], axis=1)
    got = [slots[0]]
    for k in range(1, LATS // 2):
        got.append(lax.ppermute(slots[k], "lat", [(i, i ^ (2 * k)) for i in range(LATS)]))
    return jnp.concatenate(got, axis=0)


def body(prediction_array, verifying_analysis, variable_penalty_factor):
    ens = lax.axis_index("ens").astype(jnp.int32).reshape(1)
    lat = lax.axis_index("lat").astype(jnp.int32).reshape(1)
    degrees = 0.25 * (np.arange(ROWS, dtype=np.float32) - (ROWS - 1) / 2.0)
    lat_weight = jnp.asarray(np.cos(np.deg2rad(degrees)).astype(np.float32)[:, None])

    msg = pl.pallas_call(
        pack_kernel,
        out_shape=shape(128, 3, RC, LANES),
        in_specs=[HBM],
        out_specs=HBM,
        scratch_shapes=[
            pltpu.VMEM((PACK, 2, CHANNELS // PACK, RC, COLS), jnp.float32),
            pltpu.VMEM((PACK, 128 // PACK, 3, RC, LANES), jnp.float32),
            pltpu.SemaphoreType.DMA((PACK,)),
            pltpu.SemaphoreType.DMA((PACK,)),
        ],
        compiler_params=grant(60),
        name="pack",
    )(prediction_array)
    got = lax.all_to_all(msg, ("ens", "lat"), 0, 0, tiled=True)
    obs_msg = pl.pallas_call(
        pack_obs_kernel,
        out_shape=shape(LATS, 2, RC, LANES),
        in_specs=[SMEM, VMEM],
        out_specs=VMEM,
        compiler_params=grant(2),
        name="pack_obs",
    )(lat, verifying_analysis)
    obs_got = exchange_slots(obs_msg)
    bf = jnp.bfloat16
    matrices = pl.pallas_call(
        matrices_kernel,
        out_shape=(
            shape(3 * LANES, 2 * LANES, dtype=bf),
            shape(6 * LANES, 2 * LANES, dtype=bf),
            shape(6 * LANES, 2 * LANES, dtype=bf),
            shape(6 * LANES, 2 * LANES, dtype=bf),
            shape(6 * LANES, LANES, dtype=bf),
        ),
        in_specs=[SMEM],
        out_specs=(VMEM,) * 5,
        compiler_params=grant(4),
        cost_estimate=pl.CostEstimate(flops=5_000_000, bytes_accessed=2_000_000, transcendentals=0),
        name="matrices",
    )(lat)
    padded = (ROWS + 2 * PAD, LANES)
    back = pl.pallas_call(
        work_kernel,
        out_shape=shape(PAIRS, ROWS // RC, 3, RC, LANES),
        in_specs=[SMEM] * 3 + [VMEM] * 8,
        out_specs=VMEM,
        scratch_shapes=[
            pltpu.VMEM((3 * PAIRS + 2, ROWS, LANES), jnp.float32),
            pltpu.VMEM((3 * PAIRS + 2, ROWS, LANES), jnp.float32),
            pltpu.VMEM((3 * PAIRS, *padded), jnp.float32),
            pltpu.VMEM((3 * PAIRS, *padded), jnp.float32),
            pltpu.VMEM((6 * TURN, *padded), jnp.float32),
        ],
        compiler_params=grant(16),
        name="work",
    )(ens, lat, variable_penalty_factor, lat_weight, got.reshape(PAIRS, ROWS // RC, 3, RC, LANES), obs_got, *matrices)
    ret = lax.all_to_all(back.reshape(128, 3, RC, LANES), ("ens", "lat"), 0, 0, tiled=True)
    return pl.pallas_call(
        unpack_kernel,
        out_shape=shape(2, CHANNELS, RC, COLS),
        in_specs=[VMEM],
        out_specs=HBM,
        scratch_shapes=[
            pltpu.VMEM((PACK, 2, CHANNELS // PACK, RC, COLS), jnp.float32),
            pltpu.SemaphoreType.DMA((PACK,)),
        ],
        compiler_params=grant(8),
        name="unpack",
    )(ret)


def solution(mesh):
    placed = (P("ens", None, "lat", None), P("ens", "lat", None), P())
    return jax.shard_map(
        body, mesh=mesh, in_specs=placed, out_specs=P("ens", None, "lat", None), check_vma=False
    )
```

```python
import jax
import jax.numpy as jnp
import numpy as np
from jax import lax
from jax.experimental import pallas as pl
from jax.experimental.pallas import tpu as pltpu
from jax.sharding import PartitionSpec as P

MEMBERS, CHANNELS, ROWS, COLS = 16, 16, 128, 1440
BLOCKS = 8
BLOCK = COLS // BLOCKS
LANES, SIDE, HALO = 128, 64, 6
PAIRS = MEMBERS // 2
RC = 8
PAD = 8
LATS = 16
SHARE = 0.95 / (MEMBERS - 1)
FINE, COARSE = (2, 1), (20, 15, 6, 1)
FINE_SCALE, COARSE_SCALE = 16.0, 4096.0
TURN, UNROLL = 4, 4
PACK = 4
PACK_CHANNELS = (4, 5, 4, 3)
VMEM = pl.BlockSpec(memory_space=pltpu.VMEM)
HBM = pl.BlockSpec(memory_space=pltpu.HBM)
SMEM = pl.BlockSpec(memory_space=pltpu.SMEM)


def offset_of(block):
    return (BLOCK * block + LANES - HALO) % LANES


def lane_ids(shape=(RC, LANES)):
    return lax.broadcasted_iota(jnp.int32, shape, len(shape) - 1)


def column_runs(wanted):
    runs = []
    for lane, col in wanted:
        if runs:
            p, q, n = runs[-1]
            if p + n == lane and q + n == col and col % LANES:
                runs[-1] = (p, q, n + 1)
                continue
        runs.append((lane, col, 1))
    return runs


def gather_tile(load, parts, lanes):
    tile = None
    for source, p, q, n in parts:
        base = min(q // LANES * LANES, COLS - LANES)
        piece = load(source, base)
        shift = (p - (q - base)) % LANES
        if shift:
            piece = pltpu.roll(piece, shift, 1)
        tile = piece if tile is None else jnp.where((lanes >= p) & (lanes < p + n), piece, tile)
    return tile


def main_parts(source, block):
    o = offset_of(block)
    lanes = sorted(range(LANES), key=lambda j: (j + o) % LANES)
    runs = column_runs([((j + o) % LANES, (BLOCK * block - HALO + j) % COLS) for j in lanes])
    return [(source, p, q, n) for p, q, n in runs]


def side_parts(first, second, block):
    o = offset_of(block)
    parts = []
    for source, half in ((first, 0), (second, 1)):
        wanted = [
            ((r + o) % LANES, (BLOCK * block - HALO + LANES + r % SIDE) % COLS)
            for r in range(half * SIDE, (half + 1) * SIDE)
        ]
        parts += [(source, p, q, n) for p, q, n in column_runs(sorted(wanted))]
    return parts


def pack_obs_kernel(lat_ref, obs_ref, obs_msg_ref):
    lanes = lane_ids()
    me = lat_ref[0]

    def load_obs(source, base):
        return obs_ref[source, :, base : base + LANES]

    for h in range(2):
        for b in range(BLOCKS):
            slot = me ^ (h * BLOCKS + b)
            obs_msg_ref[slot, 0] = gather_tile(load_obs, main_parts(h, b), lanes)
            obs_msg_ref[slot, 1] = gather_tile(load_obs, side_parts(h, h, b), lanes)


def pack_kernel(x_ref, msg_ref, x_buf, msg_buf, in_sem, out_sem):
    lanes = lane_ids()
    starts = [sum(PACK_CHANNELS[:g]) for g in range(len(PACK_CHANNELS) + 1)]
    spans = list(zip(starts, starts[1:]))

    def fetch(g):
        first, end = spans[g]
        return pltpu.make_async_copy(x_ref.at[:, first:end], x_buf.at[:, first:end], in_sem.at[g])

    def push(g):
        rows = slice(spans[g][0] * BLOCKS, spans[g][1] * BLOCKS)
        return pltpu.make_async_copy(msg_buf.at[rows], msg_ref.at[rows], out_sem.at[g])

    for g in range(len(spans)):
        fetch(g).start()
    for g in range(len(spans)):
        fetch(g).wait()
        for c in range(*spans[g]):
            def load(source, base):
                return x_buf[source, c, :, base : base + LANES]

            for b in range(BLOCKS):
                dst = c * BLOCKS + b
                msg_buf[dst, 0] = gather_tile(load, main_parts(0, b), lanes)
                msg_buf[dst, 1] = gather_tile(load, main_parts(1, b), lanes)
                msg_buf[dst, 2] = gather_tile(load, side_parts(0, 1, b), lanes)
        push(g).start()
    for g in range(len(spans)):
        push(g).wait()


def unpack_kernel(ret_ref, out_ref, out_buf, out_sem):
    lanes = lane_ids()
    per = CHANNELS // PACK

    def push(g):
        return pltpu.make_async_copy(out_buf.at[g], out_ref.at[:, g * per : (g + 1) * per], out_sem.at[g])

    for g in range(PACK):
        for c in range(per):
            for m in range(2):
                for t in range((COLS + LANES - 1) // LANES):
                    tile = None
                    q = t * LANES
                    end = min(q + LANES, COLS)
                    while q < end:
                        b, k = q // BLOCK, q % BLOCK
                        stop = b * BLOCK + (BLOCK - SIDE if k < BLOCK - SIDE else BLOCK)
                        src = (g * per + c) * BLOCKS + b
                        if k < BLOCK - SIDE:
                            piece = ret_ref[src, m]
                        else:
                            piece = ret_ref[src, 2]
                            if m:
                                piece = pltpu.roll(piece, SIDE, 1)
                        p = q - t * LANES
                        tile = piece if tile is None else jnp.where(lanes >= p, piece, tile)
                        q = min(stop, end)
                    if end - t * LANES == LANES:
                        out_buf[g, m, c, :, t * LANES : end] = tile
                    else:
                        out_buf[g, m, c, :, t * LANES : end] = tile[:, : end - t * LANES]
        push(g).start()
    for g in range(PACK):
        push(g).wait()


def taps(distance, weights):
    value = jnp.zeros(distance.shape, jnp.float32)
    for d, w in enumerate(weights):
        value = jnp.where(distance == d, w, value)
    return value


def matrices_kernel(lat_ref, main_ref, side_ref, back_a_ref, back_b_ref, back_s_ref):
    offset = BLOCK * (lat_ref[0] & (BLOCKS - 1)) + LANES - HALO
    size = (LANES, LANES)
    row = lax.broadcasted_iota(jnp.int32, size, 0)
    col = lax.broadcasted_iota(jnp.int32, size, 1)
    turned_row = (row - offset) & (LANES - 1)
    turned_col = (col - offset) & (LANES - 1)
    far = 99

    def put(ref, start, lane, distance, weights):
        tile = taps(distance, weights).astype(jnp.bfloat16)
        for i in range(3):
            ref[start + i * LANES : start + (i + 1) * LANES, lane : lane + LANES] = tile

    valid_col = (col >= 3) & (col < LANES - 3)
    valid_row = (row >= 3) & (row < LANES - 3)
    target_pair = jnp.where(col < SIDE, col + (LANES - 3), col + (LANES - 3 - SIDE))
    upper = turned_row >= SIDE
    mixed = jnp.where(upper, turned_row, turned_row + SIDE)
    mixed_same = upper == (col < SIDE)
    source_side = jnp.where(upper, turned_row + (LANES - SIDE), turned_row + LANES)
    out_main = (turned_col >= HALO) & (turned_col < LANES - HALO)
    out_second = (turned_col >= SIDE - HALO) & (turned_col < LANES - HALO)
    target_side = jnp.where(
        out_second, turned_col + SIDE, jnp.where(turned_col < SIDE, turned_col + LANES, turned_col)
    )
    source_pair = jnp.where(row < SIDE, row + (LANES - 3), row + (LANES - 3 - SIDE))
    back_same = (row < SIDE) != out_second
    near = jnp.where(valid_row & out_main, jnp.abs(row - turned_col), far)
    cross = jnp.where(valid_row, jnp.abs(row - target_side), far)
    for s, weights in enumerate((FINE, COARSE)):
        lane, start = s * LANES, s * 3 * LANES
        put(main_ref, 0, lane, jnp.where(valid_col, jnp.abs(turned_row - col), far), weights)
        put(side_ref, 0, lane, jnp.where(mixed_same, jnp.abs(mixed - target_pair), far), weights)
        put(side_ref, 3 * LANES, lane, jnp.where(mixed_same, far, jnp.abs(source_side - target_pair)), weights)
        put(back_a_ref, start, 0, near, weights)
        put(back_a_ref, start, LANES, jnp.where(out_second, far, cross), weights)
        put(back_b_ref, start, 0, near, weights)
        put(back_b_ref, start, LANES, jnp.where(out_second, cross, far), weights)
        put(back_s_ref, start, 0, jnp.where(back_same, jnp.abs(source_pair - target_side), far), weights)


def thirds(x):
    high = x.astype(jnp.bfloat16)
    rest = x - high.astype(jnp.float32)
    middle = rest.astype(jnp.bfloat16)
    low = (rest - middle.astype(jnp.float32)).astype(jnp.bfloat16)
    return [high, middle, low]


def times(parts, matrix):
    return jnp.dot(jnp.concatenate(parts, axis=1), matrix, preferred_element_type=jnp.float32)


def fine_taps(ref, i):
    at = lambda d: ref[i, PAD + d : PAD + d + ROWS, :]
    middle = at(0)
    return (at(-1) + at(1)) + (middle + middle)


def coarse_taps(ref, i):
    at = lambda d: ref[i, PAD + d : PAD + d + ROWS, :]
    return (at(-3) + at(3)) + (at(-2) + at(2)) * COARSE[2] + (at(-1) + at(1)) * COARSE[1] + at(0) * COARSE[0]


def mirror(ref, i):
    end = PAD + ROWS
    for outside, inside in ((PAD - 2, PAD), (PAD - 3, PAD + 1), (end + 1, end - 1), (end + 2, end - 2)):
        ref[i, outside : outside + 1, :] = -ref[i, inside : inside + 1, :]


def slope(d, floor):
    return d * lax.rsqrt(d * d + floor)


def work_kernel(
    ens_ref, lat_ref, factor_ref, weight_ref, got_ref, obs_ref, main_ref, side_ref, back_a_ref, back_b_ref, back_s_ref,
    out_ref, fine_ref, coarse_ref, gfine_ref, gcoarse_ref, rows_ref,
):
    me = lat_ref[0]
    factor = factor_ref[2 * ens_ref[0] + (me >> 3)]
    offset = BLOCK * (me & (BLOCKS - 1)) + LANES - HALO
    turned = (lane_ids((ROWS, LANES)) - offset) & (LANES - 1)
    upper = turned >= SIDE
    zeros = jnp.zeros((PAD, LANES), jnp.float32)

    def clear(i, carry):
        for ref in (gfine_ref, gcoarse_ref):
            ref[i, 0:PAD, :] = zeros
            ref[i, PAD + ROWS : 2 * PAD + ROWS, :] = zeros
        return carry

    for i in range(3 * PAIRS):
        clear(i, 0)
    for i in range(rows_ref.shape[0]):
        rows_ref[i, 0:PAD, :] = zeros
        rows_ref[i, PAD + ROWS : 2 * PAD + ROWS, :] = zeros

    def keep(i, slot, both):
        rows_ref[slot, PAD : PAD + ROWS, :] = both[:, :LANES]
        fine_ref[i] = fine_taps(rows_ref, slot)
        rows_ref[slot + 1, PAD : PAD + ROWS, :] = both[:, LANES:]
        mirror(rows_ref, slot + 1)
        coarse_ref[i] = coarse_taps(rows_ref, slot + 1)

    def mix(a, b):
        return jnp.where(upper, a, pltpu.roll(b, SIDE, 1))

    def stack(values):
        return [jnp.concatenate(part, axis=0) for part in zip(*values)]

    def forward(n, carry):
        pairs = range(TURN * n, TURN * n + TURN)
        tile = lambda p, t: got_ref[p, :, t].reshape(ROWS, LANES)
        main = times(stack([thirds(tile(p, t)) for p in pairs for t in range(2)]), main_ref[...])
        side = times(
            stack([thirds(mix(tile(p, 0), tile(p, 1))) + thirds(tile(p, 2)) for p in pairs]), side_ref[...]
        )
        for q, p in enumerate(pairs):
            for t in range(2):
                r = (2 * q + t) * ROWS
                keep(3 * p + t, 2 * (3 * q + t), main[r : r + ROWS])
        for q, p in enumerate(pairs):
            keep(3 * p + 2, 2 * (3 * q + 2), side[q * ROWS : (q + 1) * ROWS])
        return carry

    for n in range(PAIRS // TURN):
        forward(n, 0)
    a, s = (jnp.concatenate([obs_ref[me ^ l, t] for l in range(LATS)], axis=0) for t in range(2))
    keep(3 * PAIRS, 0, times(thirds(a), main_ref[...]))
    keep(3 * PAIRS + 1, 2, times(thirds(mix(a, a)) + thirds(s), side_ref[...]))

    def pull_rows(start):
        here, there = pl.ds(start, RC), pl.ds(start + PAD, RC)
        row_weight = jnp.broadcast_to(weight_ref[here, :] * factor, (RC, LANES))
        for ref, gref, scale in ((fine_ref, gfine_ref, FINE_SCALE), (coarse_ref, gcoarse_ref, COARSE_SCALE)):
            floor = 0.01 * scale * scale
            weight = row_weight * (1.0 / scale)
            shared = weight * SHARE
            mains = [3 * (m // 2) + m % 2 for m in range(MEMBERS)]
            value = [ref[i, here, :] for i in mains]
            total = [None] * MEMBERS
            for m in range(MEMBERS):
                for k in range(m + 1, MEMBERS):
                    part = slope(value[m] - value[k], floor)
                    total[m] = part if total[m] is None else total[m] + part
                    total[k] = -part if total[k] is None else total[k] - part
            target = ref[3 * PAIRS, here, :]
            for m, i in enumerate(mains):
                gref[i, there, :] = weight * slope(value[m] - target, floor) - shared * total[m]

            value = [ref[3 * p + 2, here, :] for p in range(PAIRS)]
            other = [pltpu.roll(v, SIDE, 1) for v in value]
            total = [slope(value[p] - other[p], floor) for p in range(PAIRS)]
            swapped = [None] * PAIRS
            for p in range(PAIRS):
                for k in range(p + 1, PAIRS):
                    part = slope(value[p] - value[k], floor)
                    cross = slope(value[p] - other[k], floor)
                    total[p] = total[p] + (part + cross)
                    total[k] = total[k] - part
                    swapped[k] = -cross if swapped[k] is None else swapped[k] - cross
            target = ref[3 * PAIRS + 1, here, :]
            for p in range(PAIRS):
                full = total[p] if swapped[p] is None else total[p] + pltpu.roll(swapped[p], SIDE, 1)
                gref[3 * p + 2, there, :] = weight * slope(value[p] - target, floor) - shared * full

    def pull(n, carry):
        for u in range(UNROLL):
            pull_rows(pl.multiple_of(n * (UNROLL * RC) + u * RC, RC))
        return carry

    lax.fori_loop(0, ROWS // RC // UNROLL, pull, 0)

    def backward(n, carry):
        def parts(i):
            mirror(gcoarse_ref, i)
            return thirds(fine_taps(gfine_ref, i)) + thirds(coarse_taps(gcoarse_ref, i))

        pairs = [TURN * n + q for q in range(TURN)]
        first = times(stack([parts(3 * p) for p in pairs]), back_a_ref[...])
        second = times(stack([parts(3 * p + 1) for p in pairs]), back_b_ref[...])
        side = times(stack([parts(3 * p + 2) for p in pairs]), back_s_ref[...])
        side = side + first[:, LANES:] + second[:, LANES:]
        blocks = (ROWS // RC, RC, LANES)
        for q, p in enumerate(pairs):
            r = slice(q * ROWS, (q + 1) * ROWS)
            out_ref[p, :, 0] = first[r, :LANES].reshape(blocks)
            out_ref[p, :, 1] = second[r, :LANES].reshape(blocks)
            out_ref[p, :, 2] = side[r].reshape(blocks)
        return carry

    for n in range(PAIRS // TURN):
        backward(n, 0)


def shape(*dims, dtype=jnp.float32):
    return jax.ShapeDtypeStruct(dims, dtype)


def grant(mib):
    return pltpu.CompilerParams(vmem_limit_bytes=mib << 20)


def exchange_slots(slots):
    slots = slots.reshape(LATS // 2, 2, *slots.shape[1:])
    other = lax.ppermute(slots[:, 1], "lat", [(i, i ^ 1) for i in range(LATS)])
    slots = jnp.stack([slots[:, 0], other], axis=1)
    got = [slots[0]]
    for k in range(1, LATS // 2):
        got.append(lax.ppermute(slots[k], "lat", [(i, i ^ (2 * k)) for i in range(LATS)]))
    return jnp.concatenate(got, axis=0)


def body(prediction_array, verifying_analysis, variable_penalty_factor):
    ens = lax.axis_index("ens").astype(jnp.int32).reshape(1)
    lat = lax.axis_index("lat").astype(jnp.int32).reshape(1)
    degrees = 0.25 * (np.arange(ROWS, dtype=np.float32) - (ROWS - 1) / 2.0)
    lat_weight = jnp.asarray(np.cos(np.deg2rad(degrees)).astype(np.float32)[:, None])

    msg = pl.pallas_call(
        pack_kernel,
        out_shape=shape(128, 3, RC, LANES),
        in_specs=[HBM],
        out_specs=HBM,
        scratch_shapes=[
            pltpu.VMEM((2, CHANNELS, RC, COLS), jnp.float32),
            pltpu.VMEM((128, 3, RC, LANES), jnp.float32),
            pltpu.SemaphoreType.DMA((len(PACK_CHANNELS),)),
            pltpu.SemaphoreType.DMA((len(PACK_CHANNELS),)),
        ],
        compiler_params=grant(60),
        name="pack",
    )(prediction_array)
    got = lax.all_to_all(msg, ("ens", "lat"), 0, 0, tiled=True)
    obs_msg = pl.pallas_call(
        pack_obs_kernel,
        out_shape=shape(LATS, 2, RC, LANES),
        in_specs=[SMEM, VMEM],
        out_specs=VMEM,
        compiler_params=grant(2),
        name="pack_obs",
    )(lat, verifying_analysis)
    obs_got = exchange_slots(obs_msg)
    bf = jnp.bfloat16
    matrices = pl.pallas_call(
        matrices_kernel,
        out_shape=(
            shape(3 * LANES, 2 * LANES, dtype=bf),
            shape(6 * LANES, 2 * LANES, dtype=bf),
            shape(6 * LANES, 2 * LANES, dtype=bf),
            shape(6 * LANES, 2 * LANES, dtype=bf),
            shape(6 * LANES, LANES, dtype=bf),
        ),
        in_specs=[SMEM],
        out_specs=(VMEM,) * 5,
        compiler_params=grant(4),
        cost_estimate=pl.CostEstimate(flops=5_000_000, bytes_accessed=2_000_000, transcendentals=0),
        name="matrices",
    )(lat)
    padded = (ROWS + 2 * PAD, LANES)
    back = pl.pallas_call(
        work_kernel,
        out_shape=shape(PAIRS, ROWS // RC, 3, RC, LANES),
        in_specs=[SMEM] * 3 + [VMEM] * 8,
        out_specs=VMEM,
        scratch_shapes=[
            pltpu.VMEM((3 * PAIRS + 2, ROWS, LANES), jnp.float32),
            pltpu.VMEM((3 * PAIRS + 2, ROWS, LANES), jnp.float32),
            pltpu.VMEM((3 * PAIRS, *padded), jnp.float32),
            pltpu.VMEM((3 * PAIRS, *padded), jnp.float32),
            pltpu.VMEM((6 * TURN, *padded), jnp.float32),
        ],
        compiler_params=grant(16),
        name="work",
    )(ens, lat, variable_penalty_factor, lat_weight, got.reshape(PAIRS, ROWS // RC, 3, RC, LANES), obs_got, *matrices)
    ret = lax.all_to_all(back.reshape(128, 3, RC, LANES), ("ens", "lat"), 0, 0, tiled=True)
    return pl.pallas_call(
        unpack_kernel,
        out_shape=shape(2, CHANNELS, RC, COLS),
        in_specs=[VMEM],
        out_specs=HBM,
        scratch_shapes=[
            pltpu.VMEM((PACK, 2, CHANNELS // PACK, RC, COLS), jnp.float32),
            pltpu.SemaphoreType.DMA((PACK,)),
        ],
        compiler_params=grant(8),
        name="unpack",
    )(ret)


def solution(mesh):
    placed = (P("ens", None, "lat", None), P("ens", "lat", None), P())
    return jax.shard_map(
        body, mesh=mesh, in_specs=placed, out_specs=P("ens", None, "lat", None), check_vma=False
    )
```

```python
import jax
import jax.numpy as jnp
import numpy as np
from jax import lax
from jax.experimental import pallas as pl
from jax.experimental.pallas import tpu as pltpu
from jax.sharding import PartitionSpec as P

MEMBERS, CHANNELS, ROWS, COLS = 16, 16, 128, 1440
BLOCKS = 8
BLOCK = COLS // BLOCKS
LANES, SIDE, HALO = 128, 64, 6
PAIRS = MEMBERS // 2
RC = 8
PAD = 8
LATS = 16
SHARE = 0.95 / (MEMBERS - 1)
FINE, COARSE = (2, 1), (20, 15, 6, 1)
FINE_SCALE, COARSE_SCALE = 16.0, 4096.0
TURN, UNROLL = 4, 4
PACK = 4
VMEM = pl.BlockSpec(memory_space=pltpu.VMEM)
HBM = pl.BlockSpec(memory_space=pltpu.HBM)
SMEM = pl.BlockSpec(memory_space=pltpu.SMEM)


def offset_of(block):
    return (BLOCK * block + LANES - HALO) % LANES


def lane_ids(shape=(RC, LANES)):
    return lax.broadcasted_iota(jnp.int32, shape, len(shape) - 1)


def column_runs(wanted):
    runs = []
    for lane, col in wanted:
        if runs:
            p, q, n = runs[-1]
            if p + n == lane and q + n == col and col % LANES:
                runs[-1] = (p, q, n + 1)
                continue
        runs.append((lane, col, 1))
    return runs


def gather_tile(load, parts, lanes):
    tile = None
    for source, p, q, n in parts:
        base = min(q // LANES * LANES, COLS - LANES)
        piece = load(source, base)
        shift = (p - (q - base)) % LANES
        if shift:
            piece = pltpu.roll(piece, shift, 1)
        tile = piece if tile is None else jnp.where((lanes >= p) & (lanes < p + n), piece, tile)
    return tile


def main_parts(source, block):
    o = offset_of(block)
    lanes = sorted(range(LANES), key=lambda j: (j + o) % LANES)
    runs = column_runs([((j + o) % LANES, (BLOCK * block - HALO + j) % COLS) for j in lanes])
    return [(source, p, q, n) for p, q, n in runs]


def side_parts(first, second, block):
    o = offset_of(block)
    parts = []
    for source, half in ((first, 0), (second, 1)):
        wanted = [
            ((r + o) % LANES, (BLOCK * block - HALO + LANES + r % SIDE) % COLS)
            for r in range(half * SIDE, (half + 1) * SIDE)
        ]
        parts += [(source, p, q, n) for p, q, n in column_runs(sorted(wanted))]
    return parts


def pack_obs_kernel(lat_ref, obs_ref, obs_msg_ref):
    lanes = lane_ids()
    me = lat_ref[0]

    def load_obs(source, base):
        return obs_ref[source, :, base : base + LANES]

    for h in range(2):
        for b in range(BLOCKS):
            slot = me ^ (h * BLOCKS + b)
            obs_msg_ref[slot, 0] = gather_tile(load_obs, main_parts(h, b), lanes)
            obs_msg_ref[slot, 1] = gather_tile(load_obs, side_parts(h, h, b), lanes)


def pack_kernel(x_ref, msg_ref, x_buf, msg_buf, in_sem, out_sem):
    lanes = lane_ids()
    per = CHANNELS // PACK

    def fetch(g):
        return pltpu.make_async_copy(x_ref.at[:, g * per : (g + 1) * per], x_buf.at[g], in_sem.at[g])

    def push(g):
        rows = per * BLOCKS
        return pltpu.make_async_copy(msg_buf.at[g], msg_ref.at[g * rows : (g + 1) * rows], out_sem.at[g])

    for g in range(PACK):
        fetch(g).start()
    for g in range(PACK):
        fetch(g).wait()
        for c in range(per):
            def load(source, base):
                return x_buf[g, source, c, :, base : base + LANES]

            for b in range(BLOCKS):
                dst = c * BLOCKS + b
                msg_buf[g, dst, 0] = gather_tile(load, main_parts(0, b), lanes)
                msg_buf[g, dst, 1] = gather_tile(load, main_parts(1, b), lanes)
                msg_buf[g, dst, 2] = gather_tile(load, side_parts(0, 1, b), lanes)
        push(g).start()
    for g in range(PACK):
        push(g).wait()


def unpack_kernel(ret_ref, out_ref, out_buf, out_sem):
    lanes = lane_ids()
    per = CHANNELS // PACK

    def push(g):
        return pltpu.make_async_copy(out_buf.at[g], out_ref.at[:, g * per : (g + 1) * per], out_sem.at[g])

    for g in range(PACK):
        for c in range(per):
            for m in range(2):
                for t in range((COLS + LANES - 1) // LANES):
                    tile = None
                    q = t * LANES
                    end = min(q + LANES, COLS)
                    while q < end:
                        b, k = q // BLOCK, q % BLOCK
                        stop = b * BLOCK + (BLOCK - SIDE if k < BLOCK - SIDE else BLOCK)
                        src = (g * per + c) * BLOCKS + b
                        if k < BLOCK - SIDE:
                            piece = ret_ref[src, m]
                        else:
                            piece = ret_ref[src, 2]
                            if m:
                                piece = pltpu.roll(piece, SIDE, 1)
                        p = q - t * LANES
                        tile = piece if tile is None else jnp.where(lanes >= p, piece, tile)
                        q = min(stop, end)
                    if end - t * LANES == LANES:
                        out_buf[g, m, c, :, t * LANES : end] = tile
                    else:
                        out_buf[g, m, c, :, t * LANES : end] = tile[:, : end - t * LANES]
        push(g).start()
    for g in range(PACK):
        push(g).wait()


def taps(distance, weights):
    value = jnp.zeros(distance.shape, jnp.float32)
    for d, w in enumerate(weights):
        value = jnp.where(distance == d, w, value)
    return value


def matrices_kernel(lat_ref, main_ref, side_ref, back_a_ref, back_b_ref, back_s_ref):
    offset = BLOCK * (lat_ref[0] & (BLOCKS - 1)) + LANES - HALO
    size = (LANES, LANES)
    row = lax.broadcasted_iota(jnp.int32, size, 0)
    col = lax.broadcasted_iota(jnp.int32, size, 1)
    turned_row = (row - offset) & (LANES - 1)
    turned_col = (col - offset) & (LANES - 1)
    far = 99

    def put(ref, start, lane, distance, weights):
        tile = taps(distance, weights).astype(jnp.bfloat16)
        for i in range(3):
            ref[start + i * LANES : start + (i + 1) * LANES, lane : lane + LANES] = tile

    valid_col = (col >= 3) & (col < LANES - 3)
    valid_row = (row >= 3) & (row < LANES - 3)
    target_pair = jnp.where(col < SIDE, col + (LANES - 3), col + (LANES - 3 - SIDE))
    upper = turned_row >= SIDE
    mixed = jnp.where(upper, turned_row, turned_row + SIDE)
    mixed_same = upper == (col < SIDE)
    source_side = jnp.where(upper, turned_row + (LANES - SIDE), turned_row + LANES)
    out_main = (turned_col >= HALO) & (turned_col < LANES - HALO)
    out_second = (turned_col >= SIDE - HALO) & (turned_col < LANES - HALO)
    target_side = jnp.where(
        out_second, turned_col + SIDE, jnp.where(turned_col < SIDE, turned_col + LANES, turned_col)
    )
    source_pair = jnp.where(row < SIDE, row + (LANES - 3), row + (LANES - 3 - SIDE))
    back_same = (row < SIDE) != out_second
    near = jnp.where(valid_row & out_main, jnp.abs(row - turned_col), far)
    cross = jnp.where(valid_row, jnp.abs(row - target_side), far)
    for s, weights in enumerate((FINE, COARSE)):
        lane, start = s * LANES, s * 3 * LANES
        put(main_ref, 0, lane, jnp.where(valid_col, jnp.abs(turned_row - col), far), weights)
        put(side_ref, 0, lane, jnp.where(mixed_same, jnp.abs(mixed - target_pair), far), weights)
        put(side_ref, 3 * LANES, lane, jnp.where(mixed_same, far, jnp.abs(source_side - target_pair)), weights)
        put(back_a_ref, start, 0, near, weights)
        put(back_a_ref, start, LANES, jnp.where(out_second, far, cross), weights)
        put(back_b_ref, start, 0, near, weights)
        put(back_b_ref, start, LANES, jnp.where(out_second, cross, far), weights)
        put(back_s_ref, start, 0, jnp.where(back_same, jnp.abs(source_pair - target_side), far), weights)


def thirds(x):
    high = x.astype(jnp.bfloat16)
    rest = x - high.astype(jnp.float32)
    middle = rest.astype(jnp.bfloat16)
    low = (rest - middle.astype(jnp.float32)).astype(jnp.bfloat16)
    return [high, middle, low]


def times(parts, matrix):
    return jnp.dot(jnp.concatenate(parts, axis=1), matrix, preferred_element_type=jnp.float32)


def fine_taps(ref, i):
    at = lambda d: ref[i, PAD + d : PAD + d + ROWS, :]
    middle = at(0)
    return (at(-1) + at(1)) + (middle + middle)


def coarse_taps(ref, i):
    at = lambda d: ref[i, PAD + d : PAD + d + ROWS, :]
    return (at(-3) + at(3)) + (at(-2) + at(2)) * COARSE[2] + (at(-1) + at(1)) * COARSE[1] + at(0) * COARSE[0]


def mirror(ref, i):
    end = PAD + ROWS
    for outside, inside in ((PAD - 2, PAD), (PAD - 3, PAD + 1), (end + 1, end - 1), (end + 2, end - 2)):
        ref[i, outside : outside + 1, :] = -ref[i, inside : inside + 1, :]


def slope(d, floor):
    return d * lax.rsqrt(d * d + floor)


def work_kernel(
    ens_ref, lat_ref, factor_ref, weight_ref, got_ref, obs_ref, main_ref, side_ref, back_a_ref, back_b_ref, back_s_ref,
    out_ref, fine_ref, coarse_ref, gfine_ref, gcoarse_ref, rows_ref,
):
    me = lat_ref[0]
    factor = factor_ref[2 * ens_ref[0] + (me >> 3)]
    offset = BLOCK * (me & (BLOCKS - 1)) + LANES - HALO
    turned = (lane_ids((ROWS, LANES)) - offset) & (LANES - 1)
    upper = turned >= SIDE
    zeros = jnp.zeros((PAD, LANES), jnp.float32)

    def clear(i, carry):
        for ref in (gfine_ref, gcoarse_ref):
            ref[i, 0:PAD, :] = zeros
            ref[i, PAD + ROWS : 2 * PAD + ROWS, :] = zeros
        return carry

    for i in range(3 * PAIRS):
        clear(i, 0)
    for i in range(rows_ref.shape[0]):
        rows_ref[i, 0:PAD, :] = zeros
        rows_ref[i, PAD + ROWS : 2 * PAD + ROWS, :] = zeros

    def keep(i, slot, both):
        rows_ref[slot, PAD : PAD + ROWS, :] = both[:, :LANES]
        fine_ref[i] = fine_taps(rows_ref, slot)
        rows_ref[slot + 1, PAD : PAD + ROWS, :] = both[:, LANES:]
        mirror(rows_ref, slot + 1)
        coarse_ref[i] = coarse_taps(rows_ref, slot + 1)

    def mix(a, b):
        return jnp.where(upper, a, pltpu.roll(b, SIDE, 1))

    def stack(values):
        return [jnp.concatenate(part, axis=0) for part in zip(*values)]

    def forward(n, carry):
        pairs = range(TURN * n, TURN * n + TURN)
        tile = lambda p, t: got_ref[p, :, t].reshape(ROWS, LANES)
        main = times(stack([thirds(tile(p, t)) for p in pairs for t in range(2)]), main_ref[...])
        side = times(
            stack([thirds(mix(tile(p, 0), tile(p, 1))) + thirds(tile(p, 2)) for p in pairs]), side_ref[...]
        )
        for q, p in enumerate(pairs):
            for t in range(2):
                r = (2 * q + t) * ROWS
                keep(3 * p + t, 2 * (3 * q + t), main[r : r + ROWS])
        for q, p in enumerate(pairs):
            keep(3 * p + 2, 2 * (3 * q + 2), side[q * ROWS : (q + 1) * ROWS])
        return carry

    for n in range(PAIRS // TURN):
        forward(n, 0)
    a, s = (jnp.concatenate([obs_ref[me ^ l, t] for l in range(LATS)], axis=0) for t in range(2))
    keep(3 * PAIRS, 0, times(thirds(a), main_ref[...]))
    keep(3 * PAIRS + 1, 2, times(thirds(mix(a, a)) + thirds(s), side_ref[...]))

    def pull_rows(start):
        here, there = pl.ds(start, RC), pl.ds(start + PAD, RC)
        row_weight = jnp.broadcast_to(weight_ref[here, :] * factor, (RC, LANES))
        for ref, gref, scale in ((fine_ref, gfine_ref, FINE_SCALE), (coarse_ref, gcoarse_ref, COARSE_SCALE)):
            floor = 0.01 * scale * scale
            weight = row_weight * (1.0 / scale)
            shared = weight * SHARE
            mains = [3 * (m // 2) + m % 2 for m in range(MEMBERS)]
            value = [ref[i, here, :] for i in mains]
            total = [None] * MEMBERS
            for m in range(MEMBERS):
                for k in range(m + 1, MEMBERS):
                    part = slope(value[m] - value[k], floor)
                    total[m] = part if total[m] is None else total[m] + part
                    total[k] = -part if total[k] is None else total[k] - part
            target = ref[3 * PAIRS, here, :]
            for m, i in enumerate(mains):
                gref[i, there, :] = weight * slope(value[m] - target, floor) - shared * total[m]

            value = [ref[3 * p + 2, here, :] for p in range(PAIRS)]
            other = [pltpu.roll(v, SIDE, 1) for v in value]
            total = [slope(value[p] - other[p], floor) for p in range(PAIRS)]
            swapped = [None] * PAIRS
            for p in range(PAIRS):
                for k in range(p + 1, PAIRS):
                    part = slope(value[p] - value[k], floor)
                    cross = slope(value[p] - other[k], floor)
                    total[p] = total[p] + (part + cross)
                    total[k] = total[k] - part
                    swapped[k] = -cross if swapped[k] is None else swapped[k] - cross
            target = ref[3 * PAIRS + 1, here, :]
            for p in range(PAIRS):
                full = total[p] if swapped[p] is None else total[p] + pltpu.roll(swapped[p], SIDE, 1)
                gref[3 * p + 2, there, :] = weight * slope(value[p] - target, floor) - shared * full

    def pull(n, carry):
        for u in range(UNROLL):
            pull_rows(pl.multiple_of(n * (UNROLL * RC) + u * RC, RC))
        return carry

    lax.fori_loop(0, ROWS // RC // UNROLL, pull, 0)

    def backward(n, carry):
        def parts(i):
            mirror(gcoarse_ref, i)
            return thirds(fine_taps(gfine_ref, i)) + thirds(coarse_taps(gcoarse_ref, i))

        pairs = [TURN * n + q for q in range(TURN)]
        first = times(stack([parts(3 * p) for p in pairs]), back_a_ref[...])
        second = times(stack([parts(3 * p + 1) for p in pairs]), back_b_ref[...])
        side = times(stack([parts(3 * p + 2) for p in pairs]), back_s_ref[...])
        side = side + first[:, LANES:] + second[:, LANES:]
        blocks = (ROWS // RC, RC, LANES)
        for q, p in enumerate(pairs):
            r = slice(q * ROWS, (q + 1) * ROWS)
            out_ref[p, :, 0] = first[r, :LANES].reshape(blocks)
            out_ref[p, :, 1] = second[r, :LANES].reshape(blocks)
            out_ref[p, :, 2] = side[r].reshape(blocks)
        return carry

    for n in range(PAIRS // TURN):
        backward(n, 0)


def shape(*dims, dtype=jnp.float32):
    return jax.ShapeDtypeStruct(dims, dtype)


def grant(mib):
    return pltpu.CompilerParams(vmem_limit_bytes=mib << 20)


def exchange_slots(slots):
    slots = slots.reshape(LATS // 2, 2, *slots.shape[1:])
    other = lax.ppermute(slots[:, 1], "lat", [(i, i ^ 1) for i in range(LATS)])
    slots = jnp.stack([slots[:, 0], other], axis=1)
    got = [slots[0]]
    for k in range(1, LATS // 2):
        got.append(lax.ppermute(slots[k], "lat", [(i, i ^ (2 * k)) for i in range(LATS)]))
    return jnp.concatenate(got, axis=0)


def body(prediction_array, verifying_analysis, variable_penalty_factor):
    ens = lax.axis_index("ens").astype(jnp.int32).reshape(1)
    lat = lax.axis_index("lat").astype(jnp.int32).reshape(1)
    degrees = 0.25 * (np.arange(ROWS, dtype=np.float32) - (ROWS - 1) / 2.0)
    lat_weight = jnp.asarray(np.cos(np.deg2rad(degrees)).astype(np.float32)[:, None])

    msg = pl.pallas_call(
        pack_kernel,
        out_shape=shape(128, 3, RC, LANES),
        in_specs=[HBM],
        out_specs=HBM,
        scratch_shapes=[
            pltpu.VMEM((PACK, 2, CHANNELS // PACK, RC, COLS), jnp.float32),
            pltpu.VMEM((PACK, 128 // PACK, 3, RC, LANES), jnp.float32),
            pltpu.SemaphoreType.DMA((PACK,)),
            pltpu.SemaphoreType.DMA((PACK,)),
        ],
        compiler_params=grant(60),
        name="pack",
    )(prediction_array)
    got = lax.all_to_all(msg, ("ens", "lat"), 0, 0, tiled=True)
    obs_msg = pl.pallas_call(
        pack_obs_kernel,
        out_shape=shape(LATS, 2, RC, LANES),
        in_specs=[SMEM, VMEM],
        out_specs=VMEM,
        compiler_params=grant(2),
        name="pack_obs",
    )(lat, verifying_analysis)
    obs_got = exchange_slots(obs_msg)
    bf = jnp.bfloat16
    matrices = pl.pallas_call(
        matrices_kernel,
        out_shape=(
            shape(3 * LANES, 2 * LANES, dtype=bf),
            shape(6 * LANES, 2 * LANES, dtype=bf),
            shape(6 * LANES, 2 * LANES, dtype=bf),
            shape(6 * LANES, 2 * LANES, dtype=bf),
            shape(6 * LANES, LANES, dtype=bf),
        ),
        in_specs=[SMEM],
        out_specs=(VMEM,) * 5,
        compiler_params=grant(4),
        cost_estimate=pl.CostEstimate(flops=5_000_000, bytes_accessed=2_000_000, transcendentals=0),
        name="matrices",
    )(lat)
    padded = (ROWS + 2 * PAD, LANES)
    back = pl.pallas_call(
        work_kernel,
        out_shape=shape(PAIRS, ROWS // RC, 3, RC, LANES),
        in_specs=[SMEM] * 3 + [VMEM] * 8,
        out_specs=VMEM,
        scratch_shapes=[
            pltpu.VMEM((3 * PAIRS + 2, ROWS, LANES), jnp.float32),
            pltpu.VMEM((3 * PAIRS + 2, ROWS, LANES), jnp.float32),
            pltpu.VMEM((3 * PAIRS, *padded), jnp.float32),
            pltpu.VMEM((3 * PAIRS, *padded), jnp.float32),
            pltpu.VMEM((6 * TURN, *padded), jnp.float32),
        ],
        compiler_params=grant(16),
        name="work",
    )(ens, lat, variable_penalty_factor, lat_weight, got.reshape(PAIRS, ROWS // RC, 3, RC, LANES), obs_got, *matrices)
    ret = lax.all_to_all(back.reshape(128, 3, RC, LANES), ("ens", "lat"), 0, 0, tiled=True)
    return pl.pallas_call(
        unpack_kernel,
        out_shape=shape(2, CHANNELS, RC, COLS),
        in_specs=[VMEM],
        out_specs=HBM,
        scratch_shapes=[
            pltpu.VMEM((PACK, 2, CHANNELS // PACK, RC, COLS), jnp.float32),
            pltpu.SemaphoreType.DMA((PACK,)),
        ],
        compiler_params=grant(8),
        name="unpack",
    )(ret)


def solution(mesh):
    placed = (P("ens", None, "lat", None), P("ens", "lat", None), P())
    return jax.shard_map(
        body, mesh=mesh, in_specs=placed, out_specs=P("ens", None, "lat", None), check_vma=False
    )
```
